128 devices in a mesh: row: 16 (over y, z), col: 8 (over x, core).
Axes of the slice: x: 4, y: 4, z: 4, core: 2. Of those that a mesh axis runs over, the one named last changes fastest.
Arguments:
- feats: bfloat16 [64, 32, 128, 512], P('row', 'col'), may hold values from -20 to 20
- virt_emb: bfloat16 [4, 512], replicated, may hold values from -18 to 18
- w_query: bfloat16 [512, 512], replicated, may hold values from -1 to 1
- w_key: bfloat16 [512, 512], replicated, may hold values from -1 to 1
- w_value: bfloat16 [512, 512], replicated, may hold values from -0.25 to 0.25
- w_out: bfloat16 [512, 512], replicated, may hold values from -0.25 to 0.25
- link_mask: int32 [64, 32, 4], P('row', 'col'), may hold values 0 or 1
- partners: int32 [64, 32, 4], P('row', 'col'), may hold values from 0 to 2047, as said below
- virt_ids: int32 [64, 32, 128], P('row', 'col'), may hold values from 0 to 3
Outputs:
- node_out: bfloat16 [64, 32, 128, 512], P('row', 'col')
- virt_out: float32 [4, 512], replicated
The draws below stay inside these ranges and needn't reach their ends.
Inputs may be any that keep to these rules, and one draw needn't show every extreme that they name: For every m, partners[., ., m] is a perfect matching of the blocks: the partner of a block lies on another device, and the partner's entry for m names the block back. Counted over all 4 matchings, the blocks of one device have at most 1 partners on any one device, and exactly 1 on some device.
All inputs are finite; a program needn't handle non-finite values. No bound on the sum of `link_mask` on one device may be relied on, other than what follows from the above.
Results may differ from the reference program's by a relative error of at most 0.0077.
Values may be sent and summed in bfloat16 or wider, within the bound.
A program may use at most 192 MiB of HBM per device.

```python
import math
import jax
import jax.numpy as jnp
from jax import lax

D = 512
H = 8
HD = 64
BLK = 128
BX = 4
BY = 4
NEXP = 4
NVIRT = 4
GBX = 64
GBY = 32


def virtual_table(key):
    return jax.random.randint(jax.random.fold_in(key, 7), (GBX, GBY, BLK), 0, NVIRT).astype(jnp.int32)


def virtual_base(key):
    return jax.random.normal(jax.random.fold_in(key, 5), (NVIRT, D), jnp.float32)


def query_base(key):
    return jnp.clip(jax.random.normal(jax.random.fold_in(key, 3), (D, D), jnp.float32), -4.0, 4.0) / math.sqrt(D)


def draw_virt_ids(key, part):
    return virtual_table(key)


def draw_virt_emb(key, part):
    base = virtual_base(key)
    return jnp.clip(base, -4.0, 4.0).astype(jnp.bfloat16)


def draw_w_query(key, part):
    return query_base(key).astype(jnp.bfloat16)


def draw_w_key(key, part):
    other = jnp.clip(jax.random.normal(jax.random.fold_in(key, 4), (D, D), jnp.float32), -4.0, 4.0) / math.sqrt(D)
    return other.astype(jnp.bfloat16)


def draw_feats(key, part):
    shape = (GBX, GBY, BLK, D)
    column_scales = 0.3 * jnp.exp(math.log(10.0) * jax.random.uniform(jax.random.fold_in(key, 1), (1, 1, 1, D), jnp.float32))
    return (jnp.clip(jax.random.normal(jax.random.fold_in(key, 2), shape, jnp.float32), -4.0, 4.0) * column_scales).astype(jnp.bfloat16)


def draw_partners(key, part):
    grid_rows = GBX // BX
    grid_cols = GBY // BY
    devices = grid_rows * grid_cols
    nblocks = BX * BY
    slot_count = nblocks * NEXP
    labels = jax.random.permutation(jax.random.fold_in(key, 11), devices).astype(jnp.int32)
    inverse = jnp.zeros((devices,), jnp.int32).at[labels].set(jnp.arange(devices, dtype=jnp.int32))
    masks = 1 + jax.random.permutation(jax.random.fold_in(key, 12), slot_count).astype(jnp.int32) % (devices - 1)
    first = lax.broadcasted_iota(jnp.int32, (GBX, GBY, NEXP), 0)
    second = lax.broadcasted_iota(jnp.int32, (GBX, GBY, NEXP), 1)
    matching = lax.broadcasted_iota(jnp.int32, (GBX, GBY, NEXP), 2)
    device = first // BX * grid_cols + second // BY
    slot_index = matching * nblocks + first % BX * BY + second % BY
    other = inverse[jnp.bitwise_xor(labels[device], masks[slot_index])]
    return ((other // grid_cols * BX + first % BX) * GBY + other % grid_cols * BY + second % BY).astype(jnp.int32)


def place_ends(drawn, stream_key, smallest, top_value):
    longest = drawn.shape.index(max(drawn.shape))
    spots = []
    for shift in (0, 1):
        where = [jax.random.randint(jax.random.fold_in(stream_key, axis), (), 0, length) for axis, length in enumerate(drawn.shape)]
        where[longest] = (where[longest] + shift) % drawn.shape[longest]
        spots.append(tuple(where))
    return drawn.at[spots[0]].set(smallest).at[spots[1]].set(top_value)


def scatter_about(own_key, shape, spread, bound, kind=jnp.bfloat16):
    values = spread * jax.random.normal(own_key, shape, jnp.float32)
    return jnp.clip(values, min=-bound, max=bound).astype(kind)


def setup_inputs(seed: int = 0) -> dict:
    keys = jax.random.split(jax.random.key(seed), 10)
    feats = draw_feats(jax.random.fold_in(keys[9], 71), 0)
    virt_emb = draw_virt_emb(jax.random.fold_in(keys[9], 71), 0)
    w_query = draw_w_query(jax.random.fold_in(keys[9], 71), 0)
    w_key = draw_w_key(jax.random.fold_in(keys[9], 71), 0)
    w_value = scatter_about(keys[4], (D, D), D ** -0.5, 0.25)
    w_out = scatter_about(keys[5], (D, D), D ** -0.5, 0.25)
    link_mask = place_ends((jax.random.randint(keys[6], (GBX, GBY, 4), 0, 4) < 3).astype(jnp.int32), jax.random.fold_in(keys[6], 1), 0, 1)
    partners = draw_partners(jax.random.fold_in(keys[9], 71), 0)
    virt_ids = draw_virt_ids(jax.random.fold_in(keys[9], 71), 0)
    return {"feats": feats, "virt_emb": virt_emb, "w_query": w_query, "w_key": w_key, "w_value": w_value, "w_out": w_out, "link_mask": link_mask, "partners": partners, "virt_ids": virt_ids}


NEG_FILL = -1e+30

def project_rows(matrix, weight):
    return jnp.dot(matrix, weight, preferred_element_type=jnp.float32).astype(jnp.bfloat16)

def reference(feats, virt_emb, w_query, w_key, w_value, w_out, link_mask, partners, virt_ids):
    scale = 1.0 / math.sqrt(HD)
    flat = feats.reshape(GBX * GBY * BLK, D)
    queries = project_rows(flat, w_query).reshape(GBX, GBY, BLK, H, HD)
    key_grid = project_rows(flat, w_key).reshape(GBX, GBY, BLK, H, HD)
    value_grid = project_rows(flat, w_value).reshape(GBX, GBY, BLK, H, HD)
    key_list = key_grid.reshape(GBX * GBY, BLK, H, HD)
    value_list = value_grid.reshape(GBX * GBY, BLK, H, HD)
    virtual_query = project_rows(virt_emb, w_query).astype(jnp.float32).reshape(NVIRT, H, HD)
    virtual_keys = project_rows(virt_emb, w_key).astype(jnp.float32).reshape(NVIRT, H, HD)
    virtual_values = project_rows(virt_emb, w_value).astype(jnp.float32).reshape(NVIRT, H, HD)
    columns = jnp.arange(GBY, dtype=jnp.int32)
    key_count = (5 + NEXP) * BLK

    def neighbours(grid, grid_row):
        here = lax.dynamic_index_in_dim(grid, grid_row, 0, keepdims=False)
        upper = lax.dynamic_index_in_dim(grid, jnp.maximum(grid_row - 1, 0), 0, keepdims=False)
        lower = lax.dynamic_index_in_dim(grid, jnp.minimum(grid_row + 1, GBX - 1), 0, keepdims=False)
        return [here, upper, lower, jnp.roll(here, 1, axis=0), jnp.roll(here, -1, axis=0)]

    def node_row(grid_row):
        links = lax.dynamic_index_in_dim(link_mask, grid_row, 0, keepdims=False) == 1
        chosen = lax.dynamic_index_in_dim(partners, grid_row, 0, keepdims=False)
        live = jnp.concatenate([jnp.ones((GBY, 1), bool), (links[:, 0] & (grid_row > 0))[:, None], (links[:, 1] & (grid_row < GBX - 1))[:, None], (links[:, 2] & (columns > 0))[:, None], (links[:, 3] & (columns < GBY - 1))[:, None], jnp.ones((GBY, NEXP), bool)], axis=1)
        key_sets = jnp.concatenate([jnp.stack(neighbours(key_grid, grid_row), axis=1), key_list[chosen]], axis=1)
        value_sets = jnp.concatenate([jnp.stack(neighbours(value_grid, grid_row), axis=1), value_list[chosen]], axis=1)
        key_flat = key_sets.reshape(GBY, key_count, H, HD).astype(jnp.float32)
        value_flat = value_sets.reshape(GBY, key_count, H, HD).astype(jnp.float32)
        query_row = lax.dynamic_index_in_dim(queries, grid_row, 0, keepdims=False).astype(jnp.float32)
        scores = jnp.einsum('bqhd,bkhd->bhqk', query_row, key_flat) * scale
        key_live = jnp.repeat(live, BLK, axis=1)
        scores = jnp.where(key_live[:, None, None, :], scores, NEG_FILL)
        node_ids = lax.dynamic_index_in_dim(virt_ids, grid_row, 0, keepdims=False)
        virtual_score = jnp.transpose(lax.optimization_barrier(jnp.sum(query_row * virtual_keys[node_ids], axis=-1)), (0, 2, 1)) * scale
        top = jnp.maximum(lax.optimization_barrier(jnp.max(scores, axis=-1)), virtual_score)
        shares = jnp.exp(scores - top[..., None])
        virtual_share = jnp.exp(virtual_score - top)
        total = lax.optimization_barrier(jnp.sum(shares, axis=-1)) + virtual_share
        weights = (shares / total[..., None]).astype(jnp.bfloat16)
        virtual_weight = (virtual_share / total).astype(jnp.bfloat16)
        context = jnp.einsum('bhqk,bkhd->bqhd', weights.astype(jnp.float32), value_flat)
        context = context + jnp.transpose(virtual_weight.astype(jnp.float32), (0, 2, 1))[..., None] * virtual_values[node_ids]
        context = context.astype(jnp.bfloat16).reshape(GBY * BLK, D)
        residual = lax.dynamic_index_in_dim(feats, grid_row, 0, keepdims=False).reshape(GBY * BLK, D).astype(jnp.float32)
        mixed = residual + jnp.dot(context, w_out, preferred_element_type=jnp.float32)
        return mixed.astype(jnp.bfloat16).reshape(GBY, BLK, D)
    node_out = lax.map(node_row, jnp.arange(GBX, dtype=jnp.int32))

    def virtual_row(grid_row):
        node_keys = lax.dynamic_index_in_dim(key_grid, grid_row, 0, keepdims=False).astype(jnp.float32).reshape(GBY * BLK, H, HD)
        return jnp.einsum('vhd,nhd->vhn', virtual_query, node_keys) * scale
    all_scores = lax.map(virtual_row, jnp.arange(GBX, dtype=jnp.int32))
    slots_v = jnp.arange(NVIRT, dtype=jnp.int32)
    membership = virt_ids.reshape(GBX, 1, 1, GBY * BLK) == slots_v[None, :, None, None]
    all_scores = jnp.where(membership, all_scores, NEG_FILL)
    own_score = lax.optimization_barrier(jnp.sum(virtual_query * virtual_keys, axis=-1)) * scale
    top = jnp.maximum(lax.optimization_barrier(jnp.max(all_scores, axis=(0, 3))), own_score)

    def virtual_sums(carry, grid_row):
        total, accum = carry
        row_scores = lax.dynamic_index_in_dim(all_scores, grid_row, 0, keepdims=False)
        row_members = lax.dynamic_index_in_dim(membership, grid_row, 0, keepdims=False)
        shares = jnp.where(row_members, jnp.exp(row_scores - top[..., None]), 0.0)
        row_values = lax.dynamic_index_in_dim(value_grid, grid_row, 0, keepdims=False).astype(jnp.float32).reshape(GBY * BLK, H, HD)
        accum = accum + jnp.einsum('vhn,nhd->vhd', shares, row_values, precision=lax.Precision.HIGHEST)
        return ((total + lax.optimization_barrier(jnp.sum(shares, axis=-1)), accum), None)
    start = (jnp.zeros((NVIRT, H), jnp.float32), jnp.zeros((NVIRT, H, HD), jnp.float32))
    (total, accum), _ = lax.scan(virtual_sums, start, jnp.arange(GBX, dtype=jnp.int32))
    own_share = jnp.exp(own_score - top)
    total = total + own_share
    accum = accum + own_share[..., None] * virtual_values
    virtual_context = (accum / total[..., None]).astype(jnp.bfloat16).reshape(NVIRT, D)
    virt_out = virt_emb.astype(jnp.float32) + jnp.dot(virtual_context, w_out, preferred_element_type=jnp.float32)
    return (node_out, virt_out)
```

```python
import functools
import math

import jax
import jax.numpy as jnp
from jax import lax
from jax.experimental import pallas as pl
from jax.experimental.pallas import tpu as pltpu
from jax.sharding import PartitionSpec as P


D = 512
H = 8
HD = 64
BLK = 128
NEXP = 4
NVIRT = 4
PAIRS = H // 2
NEG_FILL = -1e30
SPLIT = (96, 32)
AXES = ("row", "col")
F32 = jnp.float32
BF16 = jnp.bfloat16


def dot_nt(a, b):
    return lax.dot_general(a, b, (((1,), (1,)), ((), ())), preferred_element_type=F32)


def dot_nn(a, b):
    return jnp.dot(a, b, preferred_element_type=F32)


def device_of(partner, blocks_x, blocks_y, mesh_cols):
    grid_cols = blocks_y * mesh_cols
    return partner // grid_cols // blocks_x * mesh_cols + partner % grid_cols // blocks_y


def send_kernel(blocks_y, where_to, partners, feats, *refs):
    nblocks = feats.shape[0]
    outs, (held, in_sem, out_sems) = refs[: len(SPLIT)], refs[len(SPLIT) :]
    pltpu.make_async_copy(feats, held, in_sem).start()
    pltpu.make_async_copy(feats, held, in_sem).wait()
    first = 0
    for part, rows in enumerate(SPLIT):
        for m in range(NEXP):
            for block in range(nblocks):
                dest = where_to(partners[block // blocks_y, block % blocks_y, m])
                pltpu.make_async_copy(
                    held.at[block, pl.ds(first, rows)], outs[part].at[dest], out_sems.at[part]
                ).start()
        first += rows
    for part in range(len(SPLIT)):
        every = outs[part].at[pl.ds(0, nblocks * NEXP)]
        pltpu.make_async_copy(every, every, out_sems.at[part]).wait()


def pair_query(query_t, pair):
    both = query_t[pair * 2 * HD : (pair + 1) * 2 * HD, :]
    upper = lax.broadcasted_iota(jnp.int32, both.shape, 0) < HD
    zero = jnp.zeros_like(both)
    return jnp.concatenate([jnp.where(upper, both, zero), jnp.where(upper, zero, both)], axis=1)


def diagonal(mixed):
    return mixed[:HD, :BLK], mixed[HD:, BLK:]


def project_keys(rows, w_key, w_value_t, keys, values_t):
    gathered = rows[...]
    keys[...] = dot_nn(gathered, w_key[...]).astype(BF16)
    values_t[...] = dot_nt(w_value_t[...], gathered).astype(BF16)


def local_kernel(
    live, own, up, down, left, right, ids, w_query_t, w_key, w_value_t, virt_key, virt_value_t,
    virt_query, query_out, acc_out, top_out, total_out, virt_out, rows, keys, values_t,
    virt_top, virt_total, virt_acc,
):
    step = pl.program_id(0)
    sources = (own, up, down, left, right)
    for slot, source in enumerate(sources):
        rows[slot * BLK : (slot + 1) * BLK, :] = source[0]
    project_keys(rows, w_key, w_value_t, keys, values_t)
    query_t = (dot_nt(w_query_t[...], own[0]) * (1.0 / math.sqrt(HD))).astype(BF16)
    query_out[0] = query_t
    chosen = ids[0]
    chosen_pair = jnp.concatenate([chosen, chosen], axis=1)
    for pair in range(PAIRS):
        lanes = slice(pair * 2 * HD, (pair + 1) * 2 * HD)
        query = pair_query(query_t, pair)
        scores = dot_nn(keys[:, lanes], query)
        pieces = [scores[:BLK]]
        for slot in range(1, 5):
            alive = live[step // 4, step % 4, slot - 1] == 1
            pieces.append(jnp.where(alive, scores[slot * BLK : (slot + 1) * BLK], NEG_FILL))
        virt_scores = dot_nn(virt_key[:, lanes], query)
        member = lax.broadcasted_iota(jnp.int32, virt_scores.shape, 0) == chosen_pair
        virt_scores = jnp.where(member, virt_scores, NEG_FILL)
        top = jnp.max(virt_scores, axis=0, keepdims=True)
        for piece in pieces:
            top = jnp.maximum(top, jnp.max(piece, axis=0, keepdims=True))
        virt_shares = jnp.exp(virt_scores - top)
        total = jnp.sum(virt_shares, axis=0, keepdims=True)
        mixed = dot_nn(virt_value_t[lanes, :], virt_shares.astype(BF16))
        shares = [jnp.exp(piece - top) for piece in pieces]
        for share in shares:
            total = total + jnp.sum(share, axis=0, keepdims=True)
        weights = jnp.concatenate([share.astype(BF16) for share in shares], axis=0)
        mixed = mixed + dot_nn(values_t[lanes, :], weights)
        for half, part in enumerate(diagonal(mixed)):
            head = 2 * pair + half
            acc_out[0, head * HD : (head + 1) * HD, :] = part
            top_out[0, head : head + 1, :] = top[:, half * BLK : (half + 1) * BLK]
            total_out[0, head : head + 1, :] = total[:, half * BLK : (half + 1) * BLK]

    @pl.when(step == 0)
    def _():
        virt_top[...] = jnp.full_like(virt_top, NEG_FILL)
        virt_total[...] = jnp.zeros_like(virt_total)
        virt_acc[...] = jnp.zeros_like(virt_acc)

    scores = dot_nt(virt_query[...], keys[:BLK, :])
    member = lax.broadcasted_iota(jnp.int32, scores.shape, 0) // H == chosen
    scores = jnp.where(member, scores, NEG_FILL)
    before = virt_top[:, :1]
    top = jnp.maximum(before, jnp.max(scores, axis=1, keepdims=True))
    fade = jnp.exp(before - top)
    shares = jnp.where(member, jnp.exp(scores - top), 0.0)
    virt_top[...] = jnp.broadcast_to(top, virt_top.shape)
    virt_total[...] = virt_total[...] * fade + jnp.sum(shares, axis=1, keepdims=True)
    values = values_t[:, :BLK]
    gained = virt_acc[...] * fade
    for _ in range(3):
        rounded = shares.astype(BF16)
        gained = gained + dot_nt(rounded, values)
        shares = shares - rounded.astype(F32)
    virt_acc[...] = gained

    @pl.when(step == pl.num_programs(0) - 1)
    def _():
        head_of_lane = lax.broadcasted_iota(jnp.int32, (H, D), 1) // HD
        own_head = head_of_lane == lax.broadcasted_iota(jnp.int32, (H, D), 0)
        for v in range(NVIRT):
            heads = slice(v * H, (v + 1) * H)
            for kind, held in enumerate(
                (
                    jnp.broadcast_to(virt_top[heads, :1], (H, D)),
                    jnp.broadcast_to(virt_total[heads, :1], (H, D)),
                    virt_acc[heads, :],
                )
            ):
                row = kind * NVIRT + v
                virt_out[row : row + 1, :] = jnp.sum(
                    jnp.where(own_head, held, 0.0), axis=0, keepdims=True
                )


def remote_kernel(last, partners, *refs):
    sources, refs = refs[:NEXP], refs[NEXP:]
    query_in, acc_in, top_in, total_in, w_key, w_value_t = refs[:6]
    refs = refs[6:]
    if last:
        feats, w_out, node_out, rows, keys, values_t, context = refs
    else:
        acc_out, top_out, total_out, rows, keys, values_t = refs
    count = sources[0].shape[1]
    for slot, source in enumerate(sources):
        rows[slot * count : (slot + 1) * count, :] = source[0]
    project_keys(rows, w_key, w_value_t, keys, values_t)
    query_t = query_in[0]
    for pair in range(PAIRS):
        lanes = slice(pair * 2 * HD, (pair + 1) * 2 * HD)
        query = pair_query(query_t, pair)
        scores = dot_nn(keys[:, lanes], query)
        pick = slice(2 * pair, 2 * pair + 1)
        pick_next = slice(2 * pair + 1, 2 * pair + 2)
        before = jnp.concatenate([top_in[0, pick, :], top_in[0, pick_next, :]], axis=1)
        total = jnp.concatenate([total_in[0, pick, :], total_in[0, pick_next, :]], axis=1)
        top = jnp.maximum(before, jnp.max(scores, axis=0, keepdims=True))
        fade = jnp.exp(before - top)
        shares = jnp.exp(scores - top)
        total = total * fade + jnp.sum(shares, axis=0, keepdims=True)
        mixed = dot_nn(values_t[lanes, :], shares.astype(BF16))
        for half, part in enumerate(diagonal(mixed)):
            head = 2 * pair + half
            nodes = slice(half * BLK, (half + 1) * BLK)
            features = slice(head * HD, (head + 1) * HD)
            gained = acc_in[0, features, :] * fade[:, nodes] + part
            if last:
                context[features, :] = (gained / total[:, nodes]).astype(BF16)
            else:
                acc_out[0, features, :] = gained
                top_out[0, head : head + 1, :] = top[:, nodes]
                total_out[0, head : head + 1, :] = total[:, nodes]
    if last:
        mixed = lax.dot_general(
            context[...], w_out[...], (((0,), (0,)), ((), ())), preferred_element_type=F32
        )
        node_out[0] = (feats[0].astype(F32) + mixed).astype(BF16)


def turn(index, stride, size, shift):
    place = index // stride % size
    return index + ((place + shift) % size - place) * stride


def in_order(parts, place):
    size = len(parts)
    ordered = []
    for source in range(size):
        chosen = parts[0]
        for shift in range(1, size):
            chosen = jnp.where((place - source) % size == shift, parts[shift], chosen)
        ordered.append(chosen)
    return ordered


def merge(parts):
    tops = [part[:NVIRT] for part in parts]
    top = functools.reduce(jnp.maximum, tops)
    fades = [jnp.exp(one - top) for one in tops]
    sums = [
        sum(part[kind * NVIRT : (kind + 1) * NVIRT] * fade for part, fade in zip(parts, fades))
        for kind in (1, 2)
    ]
    return jnp.concatenate([top, *sums], axis=0)


def halo(feats):
    count_x, count_y = lax.axis_size("row"), lax.axis_size("col")

    def shift(edge, axis, count, step):
        pairs = [(i, i + step) for i in range(count) if 0 <= i + step < count]
        return lax.ppermute(edge, axis, pairs)

    return (
        shift(feats[-1], "row", count_x, 1),
        shift(feats[0], "row", count_x, -1),
        shift(feats[:, -1], "col", count_y, 1),
        shift(feats[:, 0], "col", count_y, -1),
    )


def shards(feats, virt_emb, w_query, w_key, w_value, w_out, link_mask, partners, virt_ids):
    blocks_x, blocks_y = feats.shape[0], feats.shape[1]
    nblocks = blocks_x * blocks_y
    mesh_rows, mesh_cols = lax.axis_size("row"), lax.axis_size("col")
    devices = mesh_rows * mesh_cols
    where_to = functools.partial(
        device_of, blocks_x=blocks_x, blocks_y=blocks_y, mesh_cols=mesh_cols
    )
    flat = feats.reshape(nblocks, BLK, D)
    shapes = jax.ShapeDtypeStruct
    anywhere = pl.BlockSpec(memory_space=pl.ANY)

    edges = halo(feats)
    outgoing = pl.pallas_call(
        functools.partial(send_kernel, blocks_y, where_to),
        name="send",
        out_shape=[shapes((devices, rows, D), BF16) for rows in SPLIT],
        in_specs=[pl.BlockSpec(memory_space=pltpu.SMEM), anywhere],
        out_specs=[anywhere] * len(SPLIT),
        scratch_shapes=[
            pltpu.VMEM((nblocks, BLK, D), BF16),
            pltpu.SemaphoreType.DMA,
            pltpu.SemaphoreType.DMA((len(SPLIT),)),
        ],
        cost_estimate=pl.CostEstimate(flops=0, bytes_accessed=10 << 20, transcendentals=0),
    )(partners, flat)
    arrived = []
    for part, slots in enumerate(outgoing):
        arrived.append(lax.all_to_all(slots, AXES, split_axis=0, concat_axis=0, tiled=True))

    w_query_t, w_value_t = w_query.T, w_value.T
    scale = 1.0 / math.sqrt(HD)
    virt_rows = jnp.dot(
        virt_emb, jnp.concatenate([w_query, w_key, w_value], axis=1), preferred_element_type=F32
    ).astype(BF16)
    virt_query, virt_key, virt_value = virt_rows[:, :D], virt_rows[:, D : 2 * D], virt_rows[:, 2 * D :]
    pad_to = 8
    virt_key_rows = jnp.pad(virt_key, ((0, pad_to - NVIRT), (0, 0)))
    virt_value_cols = jnp.pad(virt_value, ((0, pad_to - NVIRT), (0, 0))).T
    head_of_lane = jnp.arange(D) // HD
    own_head = head_of_lane[None, :] == jnp.arange(H)[:, None]
    virt_query_rows = jnp.where(
        own_head[None], virt_query[:, None, :] * jnp.asarray(scale, BF16), jnp.zeros((), BF16)
    ).reshape(NVIRT * H, D)

    row_ids = lax.axis_index("row") * blocks_x + jnp.arange(blocks_x, dtype=jnp.int32)[:, None]
    col_ids = lax.axis_index("col") * blocks_y + jnp.arange(blocks_y, dtype=jnp.int32)[None, :]
    inside = jnp.stack(
        [
            jnp.broadcast_to(row_ids > 0, (blocks_x, blocks_y)),
            jnp.broadcast_to(row_ids < mesh_rows * blocks_x - 1, (blocks_x, blocks_y)),
            jnp.broadcast_to(col_ids > 0, (blocks_x, blocks_y)),
            jnp.broadcast_to(col_ids < mesh_cols * blocks_y - 1, (blocks_x, blocks_y)),
        ],
        axis=-1,
    )
    live = ((link_mask == 1) & inside).astype(jnp.int32)

    padded = jnp.concatenate([flat, *edges], axis=0)
    start_up = nblocks
    start_down = start_up + blocks_y
    start_left = start_down + blocks_y
    start_right = start_left + blocks_x

    def above(b, *_):
        return (jnp.where(b < blocks_y, start_up + b, b - blocks_y), 0, 0)

    def below(b, *_):
        near = b - (nblocks - blocks_y)
        return (jnp.where(near >= 0, start_down + near, b + blocks_y), 0, 0)

    def before(b, *_):
        return (jnp.where(b % blocks_y == 0, start_left + b // blocks_y, b - 1), 0, 0)

    def after(b, *_):
        return (jnp.where(b % blocks_y == blocks_y - 1, start_right + b // blocks_y, b + 1), 0, 0)

    def same(b, *_):
        return (b, 0, 0)

    def whole(shape):
        return pl.BlockSpec(shape, lambda b, *_: (0,) * len(shape))

    block = (1, BLK, D)
    turned = (1, D, BLK)
    stats = (1, H, BLK)
    weight = whole((D, D))
    state_shapes = [
        shapes((nblocks, D, BLK), F32), shapes((nblocks, H, BLK), F32), shapes((nblocks, H, BLK), F32)
    ]
    state_specs = [pl.BlockSpec(turned, same), pl.BlockSpec(stats, same), pl.BlockSpec(stats, same)]
    local_keys = 5 * BLK
    query_t, *state, virt_part = pl.pallas_call(
        local_kernel,
        name="local",
        out_shape=[shapes((nblocks, D, BLK), BF16), *state_shapes, shapes((3 * NVIRT, D), F32)],
        grid_spec=pltpu.PrefetchScalarGridSpec(
            num_scalar_prefetch=1,
            grid=(nblocks,),
            in_specs=[
                *(pl.BlockSpec(block, index) for index in (same, above, below, before, after)),
                pl.BlockSpec((1, 1, BLK), same),
                weight, weight, weight,
                whole((pad_to, D)), whole((D, pad_to)), whole((NVIRT * H, D)),
            ],
            out_specs=[pl.BlockSpec(turned, same), *state_specs, whole((3 * NVIRT, D))],
            scratch_shapes=[
                pltpu.VMEM((local_keys, D), BF16),
                pltpu.VMEM((local_keys, D), BF16),
                pltpu.VMEM((D, local_keys), BF16),
                pltpu.VMEM((NVIRT * H, BLK), F32),
                pltpu.VMEM((NVIRT * H, BLK), F32),
                pltpu.VMEM((NVIRT * H, D), F32),
            ],
        ),
        cost_estimate=pl.CostEstimate(
            flops=40_000_000_000, bytes_accessed=30 << 20, transcendentals=nblocks * H * BLK * local_keys
        ),
    )(
        live, padded, padded, padded, padded, padded, virt_ids.reshape(nblocks, 1, BLK),
        w_query_t, w_key, w_value_t, virt_key_rows, virt_value_cols, virt_query_rows,
    )

    def partner_block(m):
        def index(b, partner):
            return (where_to(partner[b // blocks_y, b % blocks_y, m]), 0, 0)

        return index

    node_out = None
    for part, rows in enumerate(SPLIT):
        last = part == len(SPLIT) - 1
        in_specs = [
            *(pl.BlockSpec((1, rows, D), partner_block(m)) for m in range(NEXP)),
            pl.BlockSpec(turned, same), *state_specs, weight, weight,
        ]
        operands = [*[arrived[part]] * NEXP, query_t, *state, w_key, w_value_t]
        scratch = [
            pltpu.VMEM((NEXP * rows, D), BF16),
            pltpu.VMEM((NEXP * rows, D), BF16),
            pltpu.VMEM((D, NEXP * rows), BF16),
        ]
        if last:
            in_specs += [pl.BlockSpec(block, same), weight]
            operands += [flat, w_out]
            out_shape, out_specs = shapes(flat.shape, BF16), pl.BlockSpec(block, same)
            scratch += [pltpu.VMEM((D, BLK), BF16)]
        else:
            out_shape, out_specs = state_shapes, state_specs
        result = pl.pallas_call(
            functools.partial(remote_kernel, last),
            out_shape=out_shape,
            grid_spec=pltpu.PrefetchScalarGridSpec(
                num_scalar_prefetch=1, grid=(nblocks,), in_specs=in_specs, out_specs=out_specs,
                scratch_shapes=scratch,
            ),
            cost_estimate=pl.CostEstimate(
                flops=25_000_000_000 * rows // BLK,
                bytes_accessed=20 << 20,
                transcendentals=nblocks * H * BLK * NEXP * rows,
            ),
        )(partners, *operands)
        if last:
            node_out = result
        else:
            state = result

    own_score = (
        jnp.sum((virt_query.astype(F32) * virt_key.astype(F32)).reshape(NVIRT, H, HD), axis=-1) * scale
    )
    own_score = jnp.repeat(own_score, HD, axis=1)
    part = virt_part
    ways = (("col", mesh_cols, 1, 2), ("col", mesh_cols, 2, 4), ("row", mesh_rows, 4, 4), ("row", mesh_rows, 1, 4))
    for axis, count, stride, size in ways:
        others = [
            lax.ppermute(part, axis, [(i, turn(i, stride, size, shift)) for i in range(count)])
            for shift in range(1, size)
        ]
        part = merge(in_order([part, *others], lax.axis_index(axis) // stride % size))
    own = jnp.concatenate([own_score, jnp.ones_like(own_score), virt_value.astype(F32)], axis=0)
    part = merge([part, own])
    virt_context = (part[2 * NVIRT :] / part[NVIRT : 2 * NVIRT]).astype(BF16)
    virt_out = virt_emb.astype(F32) + jnp.dot(virt_context, w_out, preferred_element_type=F32)
    return node_out.reshape(feats.shape), virt_out


def solution(mesh):
    return jax.shard_map(
        shards,
        mesh=mesh,
        in_specs=(
            P("row", "col", None, None),
            P(),
            P(),
            P(),
            P(),
            P(),
            P("row", "col", None),
            P("row", "col", None),
            P("row", "col", None),
        ),
        out_specs=(P("row", "col", None, None), P()),
        check_vma=False,
    )
```

```python
import functools
import math

import jax
import jax.numpy as jnp
from jax import lax
from jax.experimental import pallas as pl
from jax.experimental.pallas import tpu as pltpu
from jax.sharding import PartitionSpec as P


D = 512
H = 8
HD = 64
BLK = 128
NEXP = 4
NVIRT = 4
PAIRS = H // 2
NEG_FILL = -1e30
SPLIT = (64, 32, 32)
TOGETHER = (2, 4, 4)
AXES = ("row", "col")
F32 = jnp.float32
BF16 = jnp.bfloat16


def dot_nt(a, b):
    return lax.dot_general(a, b, (((1,), (1,)), ((), ())), preferred_element_type=F32)


def dot_nn(a, b):
    return jnp.dot(a, b, preferred_element_type=F32)


def device_of(partner, blocks_x, blocks_y, mesh_cols):
    grid_cols = blocks_y * mesh_cols
    return partner // grid_cols // blocks_x * mesh_cols + partner % grid_cols // blocks_y


def send_kernel(first, sides, where_to, partners, feats, *refs):
    blocks_x, blocks_y = sides
    nblocks = blocks_x * blocks_y
    out, *edges = refs[:-3]
    held, in_sem, out_sem = refs[-3:]
    rows = out.shape[1]
    span = pl.ds(0, BLK) if edges else pl.ds(first, rows)
    loads = [
        pltpu.make_async_copy(feats.at[block, span], held.at[block, span], in_sem.at[block])
        for block in range(nblocks)
    ]
    for load in loads:
        load.start()
    for block, load in enumerate(loads):
        load.wait()
        for m in range(NEXP):
            dest = where_to(partners[block // blocks_y, block % blocks_y, m])
            pltpu.make_async_copy(
                held.at[block, pl.ds(first, rows)], out.at[dest], out_sem.at[0]
            ).start()
    if edges:
        last_row, first_row, last_col, first_col = edges
        moves = [
            (held.at[pl.ds(nblocks - blocks_y, blocks_y)], last_row),
            (held.at[pl.ds(0, blocks_y)], first_row),
        ]
        for row in range(blocks_x):
            moves.append((held.at[row * blocks_y + blocks_y - 1], last_col.at[row]))
            moves.append((held.at[row * blocks_y], first_col.at[row]))
        copies = [
            pltpu.make_async_copy(kept, edge, out_sem.at[1 + index])
            for index, (kept, edge) in enumerate(moves)
        ]
        for copy in copies:
            copy.start()
        for copy in copies:
            copy.wait()
    every = out.at[pl.ds(0, nblocks * NEXP)]
    pltpu.make_async_copy(every, every, out_sem.at[0]).wait()


def pair_query(query_t, pair):
    both = query_t[pair * 2 * HD : (pair + 1) * 2 * HD, :]
    upper = lax.broadcasted_iota(jnp.int32, both.shape, 0) < HD
    zero = jnp.zeros_like(both)
    return jnp.concatenate([jnp.where(upper, both, zero), jnp.where(upper, zero, both)], axis=1)


def diagonal(mixed):
    return mixed[:HD, :BLK], mixed[HD:, BLK:]


def project_keys(rows, w_key, w_value_t, keys, values_t):
    gathered = rows[...]
    keys[...] = dot_nn(gathered, w_key[...]).astype(BF16)
    values_t[...] = dot_nt(w_value_t[...], gathered).astype(BF16)


def local_kernel(
    live, own, up, down, left, right, ids, w_query_t, w_key, w_value_t, virt_key, virt_value_t,
    virt_query, query_out, acc_out, top_out, total_out, virt_out, rows, keys, values_t,
    virt_top, virt_total, virt_acc,
):
    step = pl.program_id(0)
    sources = (own, up, down, left, right)
    for slot, source in enumerate(sources):
        rows[slot * BLK : (slot + 1) * BLK, :] = source[0]
    project_keys(rows, w_key, w_value_t, keys, values_t)
    query_t = (dot_nt(w_query_t[...], own[0]) * (1.0 / math.sqrt(HD))).astype(BF16)
    query_out[0] = query_t
    chosen = ids[0]
    chosen_pair = jnp.concatenate([chosen, chosen], axis=1)
    for pair in range(PAIRS):
        lanes = slice(pair * 2 * HD, (pair + 1) * 2 * HD)
        query = pair_query(query_t, pair)
        scores = dot_nn(keys[:, lanes], query)
        pieces = [scores[:BLK]]
        for slot in range(1, 5):
            alive = live[step // 4, step % 4, slot - 1] == 1
            pieces.append(jnp.where(alive, scores[slot * BLK : (slot + 1) * BLK], NEG_FILL))
        virt_scores = dot_nn(virt_key[:, lanes], query)
        member = lax.broadcasted_iota(jnp.int32, virt_scores.shape, 0) == chosen_pair
        virt_scores = jnp.where(member, virt_scores, NEG_FILL)
        top = jnp.max(virt_scores, axis=0, keepdims=True)
        for piece in pieces:
            top = jnp.maximum(top, jnp.max(piece, axis=0, keepdims=True))
        virt_shares = jnp.exp(virt_scores - top)
        total = jnp.sum(virt_shares, axis=0, keepdims=True)
        mixed = dot_nn(virt_value_t[lanes, :], virt_shares.astype(BF16))
        shares = [jnp.exp(piece - top) for piece in pieces]
        for share in shares:
            total = total + jnp.sum(share, axis=0, keepdims=True)
        weights = jnp.concatenate([share.astype(BF16) for share in shares], axis=0)
        mixed = mixed + dot_nn(values_t[lanes, :], weights)
        for half, part in enumerate(diagonal(mixed)):
            head = 2 * pair + half
            acc_out[0, head * HD : (head + 1) * HD, :] = part
            top_out[0, head : head + 1, :] = top[:, half * BLK : (half + 1) * BLK]
            total_out[0, head : head + 1, :] = total[:, half * BLK : (half + 1) * BLK]

    @pl.when(step == 0)
    def _():
        virt_top[...] = jnp.full_like(virt_top, NEG_FILL)
        virt_total[...] = jnp.zeros_like(virt_total)
        virt_acc[...] = jnp.zeros_like(virt_acc)

    scores = dot_nt(virt_query[...], keys[:BLK, :])
    member = lax.broadcasted_iota(jnp.int32, scores.shape, 0) // H == chosen
    scores = jnp.where(member, scores, NEG_FILL)
    before = virt_top[:, :1]
    top = jnp.maximum(before, jnp.max(scores, axis=1, keepdims=True))
    fade = jnp.exp(before - top)
    shares = jnp.where(member, jnp.exp(scores - top), 0.0)
    virt_top[...] = jnp.broadcast_to(top, virt_top.shape)
    virt_total[...] = virt_total[...] * fade + jnp.sum(shares, axis=1, keepdims=True)
    values = values_t[:, :BLK]
    gained = virt_acc[...] * fade
    for _ in range(3):
        rounded = shares.astype(BF16)
        gained = gained + dot_nt(rounded, values)
        shares = shares - rounded.astype(F32)
    virt_acc[...] = gained

    @pl.when(step == pl.num_programs(0) - 1)
    def _():
        head_of_lane = lax.broadcasted_iota(jnp.int32, (H, D), 1) // HD
        own_head = head_of_lane == lax.broadcasted_iota(jnp.int32, (H, D), 0)
        for v in range(NVIRT):
            heads = slice(v * H, (v + 1) * H)
            for kind, held in enumerate(
                (
                    jnp.broadcast_to(virt_top[heads, :1], (H, D)),
                    jnp.broadcast_to(virt_total[heads, :1], (H, D)),
                    virt_acc[heads, :],
                )
            ):
                row = kind * NVIRT + v
                virt_out[row : row + 1, :] = jnp.sum(
                    jnp.where(own_head, held, 0.0), axis=0, keepdims=True
                )


def remote_kernel(last, together, slots, table, *refs):
    masked = slots != NEXP
    step = pl.program_id(0)
    sources, refs = refs[: slots * together], refs[slots * together :]
    query_in, acc_in, top_in, total_in, w_key, w_value_t = refs[:6]
    refs = refs[6:]
    if last:
        feats, w_out, node_out, rows, keys, values_t, context = refs
    else:
        acc_out, top_out, total_out, rows, keys, values_t = refs
    count = sources[0].shape[1]
    for slot, source in enumerate(sources):
        rows[slot * count : (slot + 1) * count, :] = source[0]
    project_keys(rows, w_key, w_value_t, keys, values_t)
    for block in range(together):
        query_t = query_in[block]
        known = slice(block * slots * count, (block + 1) * slots * count)
        for pair in range(PAIRS):
            lanes = slice(pair * 2 * HD, (pair + 1) * 2 * HD)
            query = pair_query(query_t, pair)
            scores = dot_nn(keys[known, lanes], query)
            if masked:
                alive = [table[slots * (step * together + block) + slot] == 1 for slot in range(slots)]
                scores = jnp.concatenate(
                    [
                        jnp.where(alive[slot], scores[slot * count : (slot + 1) * count], NEG_FILL)
                        for slot in range(slots)
                    ],
                    axis=0,
                )
            pick = slice(2 * pair, 2 * pair + 1)
            pick_next = slice(2 * pair + 1, 2 * pair + 2)
            before = jnp.concatenate([top_in[block, pick, :], top_in[block, pick_next, :]], axis=1)
            total = jnp.concatenate(
                [total_in[block, pick, :], total_in[block, pick_next, :]], axis=1
            )
            top = jnp.maximum(before, jnp.max(scores, axis=0, keepdims=True))
            fade = jnp.exp(before - top)
            shares = jnp.exp(scores - top)
            total = total * fade + jnp.sum(shares, axis=0, keepdims=True)
            mixed = dot_nn(values_t[lanes, known], shares.astype(BF16))
            for half, part in enumerate(diagonal(mixed)):
                head = 2 * pair + half
                nodes = slice(half * BLK, (half + 1) * BLK)
                features = slice(head * HD, (head + 1) * HD)
                gained = acc_in[block, features, :] * fade[:, nodes] + part
                if last:
                    context[features, block * BLK : (block + 1) * BLK] = (
                        gained / total[:, nodes]
                    ).astype(BF16)
                else:
                    acc_out[block, features, :] = gained
                    top_out[block, head : head + 1, :] = top[:, nodes]
                    total_out[block, head : head + 1, :] = total[:, nodes]
    if last:
        mixed = lax.dot_general(
            context[...], w_out[...], (((0,), (0,)), ((), ())), preferred_element_type=F32
        )
        node_out[...] = (feats[...].astype(F32) + mixed.reshape(feats.shape)).astype(BF16)


def turn(index, stride, size, shift):
    place = index // stride % size
    return index + ((place + shift) % size - place) * stride


def in_order(parts, place):
    size = len(parts)
    ordered = []
    for source in range(size):
        chosen = parts[0]
        for shift in range(1, size):
            chosen = jnp.where((place - source) % size == shift, parts[shift], chosen)
        ordered.append(chosen)
    return ordered


def finish_kernel(*refs):
    parts, (own, virt_emb, w_out, virt_out, held) = refs[:-5], refs[-5:]
    size = len(parts)
    place = lax.rem(lax.axis_index("row"), size)
    for shift, part in enumerate(parts):
        held[lax.rem(place + (size - shift), size)] = part[...]
    every = [held.at[source] for source in range(size)] + [own]
    top = functools.reduce(jnp.maximum, [one[:NVIRT] for one in every])
    total, accum = jnp.zeros_like(top), jnp.zeros_like(top)
    for one in every:
        fade = jnp.exp(one[:NVIRT] - top)
        total = total + one[NVIRT : 2 * NVIRT] * fade
        accum = accum + one[2 * NVIRT :] * fade
    context = (accum / total).astype(BF16)
    virt_out[...] = virt_emb[...].astype(F32) + dot_nn(context, w_out[...])


def merge(parts):
    tops = [part[:NVIRT] for part in parts]
    top = functools.reduce(jnp.maximum, tops)
    fades = [jnp.exp(one - top) for one in tops]
    sums = [
        sum(part[kind * NVIRT : (kind + 1) * NVIRT] * fade for part, fade in zip(parts, fades))
        for kind in (1, 2)
    ]
    return jnp.concatenate([top, *sums], axis=0)


def halo(last_row, first_row, last_col, first_col):
    count_x, count_y = lax.axis_size("row"), lax.axis_size("col")

    def shift(edge, axis, count, step):
        pairs = [(i, i + step) for i in range(count) if 0 <= i + step < count]
        return lax.ppermute(edge, axis, pairs)

    return (
        shift(last_row, "row", count_x, 1),
        shift(first_row, "row", count_x, -1),
        shift(last_col, "col", count_y, 1),
        shift(first_col, "col", count_y, -1),
    )


def shards(feats, virt_emb, w_query, w_key, w_value, w_out, link_mask, partners, virt_ids):
    blocks_x, blocks_y = feats.shape[0], feats.shape[1]
    nblocks = blocks_x * blocks_y
    mesh_rows, mesh_cols = lax.axis_size("row"), lax.axis_size("col")
    devices = mesh_rows * mesh_cols
    where_to = functools.partial(
        device_of, blocks_x=blocks_x, blocks_y=blocks_y, mesh_cols=mesh_cols
    )
    flat = feats.reshape(nblocks, BLK, D)
    shapes = jax.ShapeDtypeStruct
    anywhere = pl.BlockSpec(memory_space=pl.ANY)

    outgoing = []
    first = 0
    for part, rows in enumerate(SPLIT):
        sides = () if part else (blocks_y, blocks_y, blocks_x, blocks_x)
        out_shape = [shapes((devices, rows, D), BF16), *(shapes((n, BLK, D), BF16) for n in sides)]
        slots, *edges = pl.pallas_call(
            functools.partial(send_kernel, first, (blocks_x, blocks_y), where_to),
            out_shape=out_shape,
            in_specs=[pl.BlockSpec(memory_space=pltpu.SMEM), anywhere],
            out_specs=[anywhere] * len(out_shape),
            scratch_shapes=[
                pltpu.VMEM((nblocks, BLK, D), BF16),
                pltpu.SemaphoreType.DMA((nblocks,)),
                pltpu.SemaphoreType.DMA((3 + 2 * blocks_x,)),
            ],
            cost_estimate=pl.CostEstimate(flops=0, bytes_accessed=10 << 20, transcendentals=0),
        )(partners, flat)
        outgoing.append(slots)
        first += rows
        if edges:
            edges_in = halo(*edges)
    arrived = []
    for part, slots in enumerate(outgoing):
        arrived.append(lax.all_to_all(slots, AXES, split_axis=0, concat_axis=0, tiled=True))

    w_query_t, w_value_t = w_query.T, w_value.T
    scale = 1.0 / math.sqrt(HD)
    virt_rows = jnp.dot(
        virt_emb, jnp.concatenate([w_query, w_key, w_value], axis=1), preferred_element_type=F32
    ).astype(BF16)
    virt_query, virt_key, virt_value = virt_rows[:, :D], virt_rows[:, D : 2 * D], virt_rows[:, 2 * D :]
    pad_to = 8
    virt_key_rows = jnp.pad(virt_key, ((0, pad_to - NVIRT), (0, 0)))
    virt_value_cols = jnp.pad(virt_value, ((0, pad_to - NVIRT), (0, 0))).T
    head_of_lane = jnp.arange(D) // HD
    own_head = head_of_lane[None, :] == jnp.arange(H)[:, None]
    virt_query_rows = jnp.where(
        own_head[None], virt_query[:, None, :] * jnp.asarray(scale, BF16), jnp.zeros((), BF16)
    ).reshape(NVIRT * H, D)

    row_ids = lax.axis_index("row") * blocks_x + jnp.arange(blocks_x, dtype=jnp.int32)[:, None]
    col_ids = lax.axis_index("col") * blocks_y + jnp.arange(blocks_y, dtype=jnp.int32)[None, :]
    inside = jnp.stack(
        [
            jnp.broadcast_to(row_ids > 0, (blocks_x, blocks_y)),
            jnp.broadcast_to(row_ids < mesh_rows * blocks_x - 1, (blocks_x, blocks_y)),
            jnp.broadcast_to(col_ids > 0, (blocks_x, blocks_y)),
            jnp.broadcast_to(col_ids < mesh_cols * blocks_y - 1, (blocks_x, blocks_y)),
        ],
        axis=-1,
    )
    live = (link_mask == 1) & inside
    at_x, at_y = jnp.arange(blocks_x)[:, None], jnp.arange(blocks_y)[None, :]
    outer = (at_x == 0, at_x == blocks_x - 1, at_y == 0, at_y == blocks_y - 1)
    far = jnp.stack([jnp.broadcast_to(side, (blocks_x, blocks_y)) for side in outer], axis=-1)
    near_live = (live & ~far).astype(jnp.int32)
    far_live = (live & far).reshape(nblocks, 2, 2).any(axis=-1).astype(jnp.int32).reshape(-1)

    def above(b, *_):
        return (jnp.where(b < blocks_y, b, b - blocks_y), 0, 0)

    def below(b, *_):
        return (jnp.where(b >= nblocks - blocks_y, b, b + blocks_y), 0, 0)

    def before(b, *_):
        return (jnp.where(b % blocks_y == 0, b, b - 1), 0, 0)

    def after(b, *_):
        return (jnp.where(b % blocks_y == blocks_y - 1, b, b + 1), 0, 0)

    def same(b, *_):
        return (b, 0, 0)

    def whole(shape):
        return pl.BlockSpec(shape, lambda b, *_: (0,) * len(shape))

    block = (1, BLK, D)
    turned = (1, D, BLK)
    stats = (1, H, BLK)
    weight = whole((D, D))
    state_shapes = [
        shapes((nblocks, D, BLK), F32), shapes((nblocks, H, BLK), F32), shapes((nblocks, H, BLK), F32)
    ]
    state_specs = [pl.BlockSpec(turned, same), pl.BlockSpec(stats, same), pl.BlockSpec(stats, same)]
    local_keys = 5 * BLK
    query_t, *state, virt_part = pl.pallas_call(
        local_kernel,
        name="local",
        out_shape=[shapes((nblocks, D, BLK), BF16), *state_shapes, shapes((3 * NVIRT, D), F32)],
        grid_spec=pltpu.PrefetchScalarGridSpec(
            num_scalar_prefetch=1,
            grid=(nblocks,),
            in_specs=[
                *(pl.BlockSpec(block, index) for index in (same, above, below, before, after)),
                pl.BlockSpec((1, 1, BLK), same),
                weight, weight, weight,
                whole((pad_to, D)), whole((D, pad_to)), whole((NVIRT * H, D)),
            ],
            out_specs=[pl.BlockSpec(turned, same), *state_specs, whole((3 * NVIRT, D))],
            scratch_shapes=[
                pltpu.VMEM((local_keys, D), BF16),
                pltpu.VMEM((local_keys, D), BF16),
                pltpu.VMEM((D, local_keys), BF16),
                pltpu.VMEM((NVIRT * H, BLK), F32),
                pltpu.VMEM((NVIRT * H, BLK), F32),
                pltpu.VMEM((NVIRT * H, D), F32),
            ],
        ),
        cost_estimate=pl.CostEstimate(
            flops=40_000_000_000, bytes_accessed=30 << 20, transcendentals=nblocks * H * BLK * local_keys
        ),
    )(
        near_live, flat, flat, flat, flat, flat, virt_ids.reshape(nblocks, 1, BLK),
        w_query_t, w_key, w_value_t, virt_key_rows, virt_value_cols, virt_query_rows,
    )

    def add_keys(source, rows, together, slots, table, index, state, finish=()):
        def blocks_of(*shape):
            return pl.BlockSpec((together, *shape), same)

        states = [blocks_of(D, BLK), blocks_of(H, BLK), blocks_of(H, BLK)]
        in_specs = [
            *(
                pl.BlockSpec((1, rows, D), functools.partial(index, together, offset, slot))
                for offset in range(together)
                for slot in range(slots)
            ),
            blocks_of(D, BLK), *states, weight, weight,
        ]
        count = together * slots * rows
        scratch = [
            pltpu.VMEM((count, D), BF16), pltpu.VMEM((count, D), BF16), pltpu.VMEM((D, count), BF16)
        ]
        if finish:
            in_specs += [blocks_of(BLK, D), weight]
            out_shape, out_specs = shapes(flat.shape, BF16), blocks_of(BLK, D)
            scratch += [pltpu.VMEM((D, together * BLK), BF16)]
        else:
            out_shape, out_specs = state_shapes, states
        return pl.pallas_call(
            functools.partial(remote_kernel, bool(finish), together, slots),
            out_shape=out_shape,
            grid_spec=pltpu.PrefetchScalarGridSpec(
                num_scalar_prefetch=1, grid=(nblocks // together,), in_specs=in_specs,
                out_specs=out_specs, scratch_shapes=scratch,
            ),
            cost_estimate=pl.CostEstimate(
                flops=50_000_000 * slots * rows,
                bytes_accessed=20 << 20,
                transcendentals=nblocks * H * BLK * slots * rows,
            ),
        )(table, *[source] * (slots * together), query_t, *state, w_key, w_value_t, *finish)

    def partner_block(together, offset, slot, b, partner):
        at = b * together + offset
        return (where_to(partner[at // blocks_y, at % blocks_y, slot]), 0, 0)

    def edge_block(together, offset, slot, b, _):
        at = b * together + offset
        row, col = at // blocks_y, at % blocks_y
        if slot == 0:
            return (jnp.where(row == blocks_x - 1, blocks_y + col, col), 0, 0)
        return (2 * blocks_y + jnp.where(col == blocks_y - 1, blocks_x + row, row), 0, 0)

    state = add_keys(arrived[0], SPLIT[0], TOGETHER[0], NEXP, partners, partner_block, state)
    edge_blocks = jnp.concatenate(edges_in, axis=0)
    state = add_keys(edge_blocks, BLK, TOGETHER[0], 2, far_live, edge_block, state)
    state = add_keys(arrived[1], SPLIT[1], TOGETHER[1], NEXP, partners, partner_block, state)
    node_out = add_keys(
        arrived[2], SPLIT[2], TOGETHER[2], NEXP, partners, partner_block, state,
        (flat, w_out),
    )

    own_score = (
        jnp.sum((virt_query.astype(F32) * virt_key.astype(F32)).reshape(NVIRT, H, HD), axis=-1) * scale
    )
    own_score = jnp.repeat(own_score, HD, axis=1)
    part = virt_part
    ways = (
        ("col", mesh_cols, 1, 2),
        ("col", mesh_cols, 2, mesh_cols // 2),
        ("row", mesh_rows, 4, mesh_rows // 4),
        ("row", mesh_rows, 1, 4),
    )
    for stage, (axis, count, stride, size) in enumerate(ways):
        parts = [part] + [
            lax.ppermute(part, axis, [(i, turn(i, stride, size, shift)) for i in range(count)])
            for shift in range(1, size)
        ]
        if stage < len(ways) - 1:
            part = merge(in_order(parts, lax.axis_index(axis) // stride % size))
    own = jnp.concatenate([own_score, jnp.ones_like(own_score), virt_value.astype(F32)], axis=0)
    virt_out = pl.pallas_call(
        finish_kernel,
        name="finish",
        out_shape=shapes((NVIRT, D), F32),
        scratch_shapes=[pltpu.VMEM((len(parts), 3 * NVIRT, D), F32)],
        cost_estimate=pl.CostEstimate(flops=1 << 21, bytes_accessed=1 << 20, transcendentals=1 << 16),
    )(*parts, own, virt_emb, w_out)
    return node_out.reshape(feats.shape), virt_out


def solution(mesh):
    return jax.shard_map(
        shards,
        mesh=mesh,
        in_specs=(
            P("row", "col", None, None),
            P(),
            P(),
            P(),
            P(),
            P(),
            P("row", "col", None),
            P("row", "col", None),
            P("row", "col", None),
        ),
        out_specs=(P("row", "col", None, None), P()),
        check_vma=False,
    )
```

```python
import functools
import math

import jax
import jax.numpy as jnp
from jax import lax
from jax.experimental import pallas as pl
from jax.experimental.pallas import tpu as pltpu
from jax.sharding import PartitionSpec as P


D = 512
H = 8
HD = 64
BLK = 128
NEXP = 4
NVIRT = 4
PAIRS = H // 2
NEG_FILL = -1e30
SPLIT = (64, 32, 32)
TOGETHER = (2, 4, 4)
AXES = ("row", "col")
F32 = jnp.float32
BF16 = jnp.bfloat16


def dot_nt(a, b):
    return lax.dot_general(a, b, (((1,), (1,)), ((), ())), preferred_element_type=F32)


def dot_nn(a, b):
    return jnp.dot(a, b, preferred_element_type=F32)


def device_of(partner, blocks_x, blocks_y, mesh_cols):
    grid_cols = blocks_y * mesh_cols
    return partner // grid_cols // blocks_x * mesh_cols + partner % grid_cols // blocks_y


def send_kernel(first, sides, where_to, partners, feats, *refs):
    blocks_x, blocks_y = sides
    nblocks = blocks_x * blocks_y
    out, *edges = refs[:-3]
    held, in_sem, out_sem = refs[-3:]
    rows = out.shape[1]
    loads = [
        pltpu.make_async_copy(feats.at[block], held.at[block], in_sem.at[block])
        for block in range(nblocks)
    ]
    for load in loads:
        load.start()
    for block, load in enumerate(loads):
        load.wait()
        for m in range(NEXP):
            dest = where_to(partners[block // blocks_y, block % blocks_y, m])
            pltpu.make_async_copy(
                held.at[block, pl.ds(first, rows)], out.at[dest], out_sem.at[0]
            ).start()
    if edges:
        last_row, first_row, last_col, first_col = edges
        moves = [
            (held.at[pl.ds(nblocks - blocks_y, blocks_y)], last_row),
            (held.at[pl.ds(0, blocks_y)], first_row),
        ]
        for row in range(blocks_x):
            moves.append((held.at[row * blocks_y + blocks_y - 1], last_col.at[row]))
            moves.append((held.at[row * blocks_y], first_col.at[row]))
        copies = [
            pltpu.make_async_copy(kept, edge, out_sem.at[1 + index])
            for index, (kept, edge) in enumerate(moves)
        ]
        for copy in copies:
            copy.start()
        for copy in copies:
            copy.wait()
    every = out.at[pl.ds(0, nblocks * NEXP)]
    pltpu.make_async_copy(every, every, out_sem.at[0]).wait()


def pair_query(query_t, pair):
    both = query_t[pair * 2 * HD : (pair + 1) * 2 * HD, :]
    upper = lax.broadcasted_iota(jnp.int32, both.shape, 0) < HD
    zero = jnp.zeros_like(both)
    return jnp.concatenate([jnp.where(upper, both, zero), jnp.where(upper, zero, both)], axis=1)


def diagonal(mixed):
    return mixed[:HD, :BLK], mixed[HD:, BLK:]


def project_keys(rows, w_key, w_value_t, keys, values_t):
    gathered = rows[...]
    keys[...] = dot_nn(gathered, w_key[...]).astype(BF16)
    values_t[...] = dot_nt(w_value_t[...], gathered).astype(BF16)


def local_kernel(
    live, own, up, down, left, right, ids, w_query_t, w_key, w_value_t, virt_key, virt_value_t,
    virt_query, query_out, acc_out, top_out, total_out, virt_out, rows, keys, values_t,
    virt_top, virt_total, virt_acc,
):
    step = pl.program_id(0)
    sources = (own, up, down, left, right)
    for slot, source in enumerate(sources):
        rows[slot * BLK : (slot + 1) * BLK, :] = source[0]
    project_keys(rows, w_key, w_value_t, keys, values_t)
    query_t = (dot_nt(w_query_t[...], own[0]) * (1.0 / math.sqrt(HD))).astype(BF16)
    query_out[0] = query_t
    chosen = ids[0]
    chosen_pair = jnp.concatenate([chosen, chosen], axis=1)
    for pair in range(PAIRS):
        lanes = slice(pair * 2 * HD, (pair + 1) * 2 * HD)
        query = pair_query(query_t, pair)
        scores = dot_nn(keys[:, lanes], query)
        pieces = [scores[:BLK]]
        for slot in range(1, 5):
            alive = live[step // 4, step % 4, slot - 1] == 1
            pieces.append(jnp.where(alive, scores[slot * BLK : (slot + 1) * BLK], NEG_FILL))
        virt_scores = dot_nn(virt_key[:, lanes], query)
        member = lax.broadcasted_iota(jnp.int32, virt_scores.shape, 0) == chosen_pair
        virt_scores = jnp.where(member, virt_scores, NEG_FILL)
        top = jnp.max(virt_scores, axis=0, keepdims=True)
        for piece in pieces:
            top = jnp.maximum(top, jnp.max(piece, axis=0, keepdims=True))
        virt_shares = jnp.exp(virt_scores - top)
        total = jnp.sum(virt_shares, axis=0, keepdims=True)
        mixed = dot_nn(virt_value_t[lanes, :], virt_shares.astype(BF16))
        shares = [jnp.exp(piece - top) for piece in pieces]
        for share in shares:
            total = total + jnp.sum(share, axis=0, keepdims=True)
        weights = jnp.concatenate([share.astype(BF16) for share in shares], axis=0)
        mixed = mixed + dot_nn(values_t[lanes, :], weights)
        for half, part in enumerate(diagonal(mixed)):
            head = 2 * pair + half
            acc_out[0, head * HD : (head + 1) * HD, :] = part
            top_out[0, head : head + 1, :] = top[:, half * BLK : (half + 1) * BLK]
            total_out[0, head : head + 1, :] = total[:, half * BLK : (half + 1) * BLK]

    @pl.when(step == 0)
    def _():
        virt_top[...] = jnp.full_like(virt_top, NEG_FILL)
        virt_total[...] = jnp.zeros_like(virt_total)
        virt_acc[...] = jnp.zeros_like(virt_acc)

    scores = dot_nt(virt_query[...], keys[:BLK, :])
    member = lax.broadcasted_iota(jnp.int32, scores.shape, 0) // H == chosen
    scores = jnp.where(member, scores, NEG_FILL)
    before = virt_top[:, :1]
    top = jnp.maximum(before, jnp.max(scores, axis=1, keepdims=True))
    fade = jnp.exp(before - top)
    shares = jnp.where(member, jnp.exp(scores - top), 0.0)
    virt_top[...] = jnp.broadcast_to(top, virt_top.shape)
    virt_total[...] = virt_total[...] * fade + jnp.sum(shares, axis=1, keepdims=True)
    values = values_t[:, :BLK]
    gained = virt_acc[...] * fade
    for _ in range(3):
        rounded = shares.astype(BF16)
        gained = gained + dot_nt(rounded, values)
        shares = shares - rounded.astype(F32)
    virt_acc[...] = gained

    @pl.when(step == pl.num_programs(0) - 1)
    def _():
        head_of_lane = lax.broadcasted_iota(jnp.int32, (H, D), 1) // HD
        own_head = head_of_lane == lax.broadcasted_iota(jnp.int32, (H, D), 0)
        for v in range(NVIRT):
            heads = slice(v * H, (v + 1) * H)
            for kind, held in enumerate(
                (
                    jnp.broadcast_to(virt_top[heads, :1], (H, D)),
                    jnp.broadcast_to(virt_total[heads, :1], (H, D)),
                    virt_acc[heads, :],
                )
            ):
                row = kind * NVIRT + v
                virt_out[row : row + 1, :] = jnp.sum(
                    jnp.where(own_head, held, 0.0), axis=0, keepdims=True
                )


def remote_kernel(last, together, slots, table, *refs):
    masked = slots != NEXP
    step = pl.program_id(0)
    sources, refs = refs[: slots * together], refs[slots * together :]
    query_in, acc_in, top_in, total_in, w_key, w_value_t = refs[:6]
    refs = refs[6:]
    if last:
        feats, w_out, node_out, rows, keys, values_t, context = refs
    else:
        acc_out, top_out, total_out, rows, keys, values_t = refs
    count = sources[0].shape[1]
    for slot, source in enumerate(sources):
        rows[slot * count : (slot + 1) * count, :] = source[0]
    project_keys(rows, w_key, w_value_t, keys, values_t)
    for block in range(together):
        query_t = query_in[block]
        known = slice(block * slots * count, (block + 1) * slots * count)
        for pair in range(PAIRS):
            lanes = slice(pair * 2 * HD, (pair + 1) * 2 * HD)
            query = pair_query(query_t, pair)
            scores = dot_nn(keys[known, lanes], query)
            if masked:
                alive = [table[slots * (step * together + block) + slot] == 1 for slot in range(slots)]
                scores = jnp.concatenate(
                    [
                        jnp.where(alive[slot], scores[slot * count : (slot + 1) * count], NEG_FILL)
                        for slot in range(slots)
                    ],
                    axis=0,
                )
            pick = slice(2 * pair, 2 * pair + 1)
            pick_next = slice(2 * pair + 1, 2 * pair + 2)
            before = jnp.concatenate([top_in[block, pick, :], top_in[block, pick_next, :]], axis=1)
            total = jnp.concatenate(
                [total_in[block, pick, :], total_in[block, pick_next, :]], axis=1
            )
            top = jnp.maximum(before, jnp.max(scores, axis=0, keepdims=True))
            fade = jnp.exp(before - top)
            shares = jnp.exp(scores - top)
            total = total * fade + jnp.sum(shares, axis=0, keepdims=True)
            mixed = dot_nn(values_t[lanes, known], shares.astype(BF16))
            for half, part in enumerate(diagonal(mixed)):
                head = 2 * pair + half
                nodes = slice(half * BLK, (half + 1) * BLK)
                features = slice(head * HD, (head + 1) * HD)
                gained = acc_in[block, features, :] * fade[:, nodes] + part
                if last:
                    context[features, block * BLK : (block + 1) * BLK] = (
                        gained / total[:, nodes]
                    ).astype(BF16)
                else:
                    acc_out[block, features, :] = gained
                    top_out[block, head : head + 1, :] = top[:, nodes]
                    total_out[block, head : head + 1, :] = total[:, nodes]
    if last:
        mixed = lax.dot_general(
            context[...], w_out[...], (((0,), (0,)), ((), ())), preferred_element_type=F32
        )
        node_out[...] = (feats[...].astype(F32) + mixed.reshape(feats.shape)).astype(BF16)


def turn(index, stride, size, shift):
    place = index // stride % size
    return index + ((place + shift) % size - place) * stride


def in_order(parts, place):
    size = len(parts)
    ordered = []
    for source in range(size):
        chosen = parts[0]
        for shift in range(1, size):
            chosen = jnp.where((place - source) % size == shift, parts[shift], chosen)
        ordered.append(chosen)
    return ordered


def finish_kernel(*refs):
    parts, (own, virt_emb, w_out, virt_out, held) = refs[:-5], refs[-5:]
    size = len(parts)
    place = lax.rem(lax.axis_index("row"), size)
    for shift, part in enumerate(parts):
        held[lax.rem(place + (size - shift), size)] = part[...]
    every = [held.at[source] for source in range(size)] + [own]
    top = functools.reduce(jnp.maximum, [one[:NVIRT] for one in every])
    total, accum = jnp.zeros_like(top), jnp.zeros_like(top)
    for one in every:
        fade = jnp.exp(one[:NVIRT] - top)
        total = total + one[NVIRT : 2 * NVIRT] * fade
        accum = accum + one[2 * NVIRT :] * fade
    context = (accum / total).astype(BF16)
    virt_out[...] = virt_emb[...].astype(F32) + dot_nn(context, w_out[...])


def merge(parts):
    tops = [part[:NVIRT] for part in parts]
    top = functools.reduce(jnp.maximum, tops)
    fades = [jnp.exp(one - top) for one in tops]
    sums = [
        sum(part[kind * NVIRT : (kind + 1) * NVIRT] * fade for part, fade in zip(parts, fades))
        for kind in (1, 2)
    ]
    return jnp.concatenate([top, *sums], axis=0)


def halo(last_row, first_row, last_col, first_col):
    count_x, count_y = lax.axis_size("row"), lax.axis_size("col")

    def shift(edge, axis, count, step):
        pairs = [(i, i + step) for i in range(count) if 0 <= i + step < count]
        return lax.ppermute(edge, axis, pairs)

    return (
        shift(last_row, "row", count_x, 1),
        shift(first_row, "row", count_x, -1),
        shift(last_col, "col", count_y, 1),
        shift(first_col, "col", count_y, -1),
    )


def shards(feats, virt_emb, w_query, w_key, w_value, w_out, link_mask, partners, virt_ids):
    blocks_x, blocks_y = feats.shape[0], feats.shape[1]
    nblocks = blocks_x * blocks_y
    mesh_rows, mesh_cols = lax.axis_size("row"), lax.axis_size("col")
    devices = mesh_rows * mesh_cols
    where_to = functools.partial(
        device_of, blocks_x=blocks_x, blocks_y=blocks_y, mesh_cols=mesh_cols
    )
    flat = feats.reshape(nblocks, BLK, D)
    shapes = jax.ShapeDtypeStruct
    anywhere = pl.BlockSpec(memory_space=pl.ANY)

    outgoing = []
    first = 0
    for part, rows in enumerate(SPLIT):
        sides = (blocks_y, blocks_y, blocks_x, blocks_x) if part == 1 else ()
        out_shape = [shapes((devices, rows, D), BF16), *(shapes((n, BLK, D), BF16) for n in sides)]
        slots, *edges = pl.pallas_call(
            functools.partial(send_kernel, first, (blocks_x, blocks_y), where_to),
            out_shape=out_shape,
            in_specs=[pl.BlockSpec(memory_space=pltpu.SMEM), anywhere],
            out_specs=[anywhere] * len(out_shape),
            scratch_shapes=[
                pltpu.VMEM((nblocks, BLK, D), BF16),
                pltpu.SemaphoreType.DMA((nblocks,)),
                pltpu.SemaphoreType.DMA((3 + 2 * blocks_x,)),
            ],
            cost_estimate=pl.CostEstimate(flops=0, bytes_accessed=10 << 20, transcendentals=0),
        )(partners, flat)
        outgoing.append(slots)
        first += rows
        if edges:
            edges_in = halo(*edges)
    arrived = []
    for part, slots in enumerate(outgoing):
        arrived.append(lax.all_to_all(slots, AXES, split_axis=0, concat_axis=0, tiled=True))

    w_query_t, w_value_t = w_query.T, w_value.T
    scale = 1.0 / math.sqrt(HD)
    virt_rows = jnp.dot(
        virt_emb, jnp.concatenate([w_query, w_key, w_value], axis=1), preferred_element_type=F32
    ).astype(BF16)
    virt_query, virt_key, virt_value = virt_rows[:, :D], virt_rows[:, D : 2 * D], virt_rows[:, 2 * D :]
    pad_to = 8
    virt_key_rows = jnp.pad(virt_key, ((0, pad_to - NVIRT), (0, 0)))
    virt_value_cols = jnp.pad(virt_value, ((0, pad_to - NVIRT), (0, 0))).T
    head_of_lane = jnp.arange(D) // HD
    own_head = head_of_lane[None, :] == jnp.arange(H)[:, None]
    virt_query_rows = jnp.where(
        own_head[None], virt_query[:, None, :] * jnp.asarray(scale, BF16), jnp.zeros((), BF16)
    ).reshape(NVIRT * H, D)

    row_ids = lax.axis_index("row") * blocks_x + jnp.arange(blocks_x, dtype=jnp.int32)[:, None]
    col_ids = lax.axis_index("col") * blocks_y + jnp.arange(blocks_y, dtype=jnp.int32)[None, :]
    inside = jnp.stack(
        [
            jnp.broadcast_to(row_ids > 0, (blocks_x, blocks_y)),
            jnp.broadcast_to(row_ids < mesh_rows * blocks_x - 1, (blocks_x, blocks_y)),
            jnp.broadcast_to(col_ids > 0, (blocks_x, blocks_y)),
            jnp.broadcast_to(col_ids < mesh_cols * blocks_y - 1, (blocks_x, blocks_y)),
        ],
        axis=-1,
    )
    live = (link_mask == 1) & inside
    at_x, at_y = jnp.arange(blocks_x)[:, None], jnp.arange(blocks_y)[None, :]
    outer = (at_x == 0, at_x == blocks_x - 1, at_y == 0, at_y == blocks_y - 1)
    far = jnp.stack([jnp.broadcast_to(side, (blocks_x, blocks_y)) for side in outer], axis=-1)
    near_live = (live & ~far).astype(jnp.int32)
    far_live = (live & far).reshape(nblocks, 2, 2).any(axis=-1).astype(jnp.int32).reshape(-1)

    def above(b, *_):
        return (jnp.where(b < blocks_y, b, b - blocks_y), 0, 0)

    def below(b, *_):
        return (jnp.where(b >= nblocks - blocks_y, b, b + blocks_y), 0, 0)

    def before(b, *_):
        return (jnp.where(b % blocks_y == 0, b, b - 1), 0, 0)

    def after(b, *_):
        return (jnp.where(b % blocks_y == blocks_y - 1, b, b + 1), 0, 0)

    def same(b, *_):
        return (b, 0, 0)

    def whole(shape):
        return pl.BlockSpec(shape, lambda b, *_: (0,) * len(shape))

    block = (1, BLK, D)
    turned = (1, D, BLK)
    stats = (1, H, BLK)
    weight = whole((D, D))
    state_shapes = [
        shapes((nblocks, D, BLK), F32), shapes((nblocks, H, BLK), F32), shapes((nblocks, H, BLK), F32)
    ]
    state_specs = [pl.BlockSpec(turned, same), pl.BlockSpec(stats, same), pl.BlockSpec(stats, same)]
    local_keys = 5 * BLK
    query_t, *state, virt_part = pl.pallas_call(
        local_kernel,
        name="local",
        out_shape=[shapes((nblocks, D, BLK), BF16), *state_shapes, shapes((3 * NVIRT, D), F32)],
        grid_spec=pltpu.PrefetchScalarGridSpec(
            num_scalar_prefetch=1,
            grid=(nblocks,),
            in_specs=[
                *(pl.BlockSpec(block, index) for index in (same, above, below, before, after)),
                pl.BlockSpec((1, 1, BLK), same),
                weight, weight, weight,
                whole((pad_to, D)), whole((D, pad_to)), whole((NVIRT * H, D)),
            ],
            out_specs=[pl.BlockSpec(turned, same), *state_specs, whole((3 * NVIRT, D))],
            scratch_shapes=[
                pltpu.VMEM((local_keys, D), BF16),
                pltpu.VMEM((local_keys, D), BF16),
                pltpu.VMEM((D, local_keys), BF16),
                pltpu.VMEM((NVIRT * H, BLK), F32),
                pltpu.VMEM((NVIRT * H, BLK), F32),
                pltpu.VMEM((NVIRT * H, D), F32),
            ],
        ),
        cost_estimate=pl.CostEstimate(
            flops=40_000_000_000, bytes_accessed=30 << 20, transcendentals=nblocks * H * BLK * local_keys
        ),
    )(
        near_live, flat, flat, flat, flat, flat, virt_ids.reshape(nblocks, 1, BLK),
        w_query_t, w_key, w_value_t, virt_key_rows, virt_value_cols, virt_query_rows,
    )

    def add_keys(source, rows, together, slots, table, index, state, finish=()):
        def blocks_of(*shape):
            return pl.BlockSpec((together, *shape), same)

        states = [blocks_of(D, BLK), blocks_of(H, BLK), blocks_of(H, BLK)]
        in_specs = [
            *(
                pl.BlockSpec((1, rows, D), functools.partial(index, together, offset, slot))
                for offset in range(together)
                for slot in range(slots)
            ),
            blocks_of(D, BLK), *states, weight, weight,
        ]
        count = together * slots * rows
        scratch = [
            pltpu.VMEM((count, D), BF16), pltpu.VMEM((count, D), BF16), pltpu.VMEM((D, count), BF16)
        ]
        if finish:
            in_specs += [blocks_of(BLK, D), weight]
            out_shape, out_specs = shapes(flat.shape, BF16), blocks_of(BLK, D)
            scratch += [pltpu.VMEM((D, together * BLK), BF16)]
        else:
            out_shape, out_specs = state_shapes, states
        return pl.pallas_call(
            functools.partial(remote_kernel, bool(finish), together, slots),
            out_shape=out_shape,
            grid_spec=pltpu.PrefetchScalarGridSpec(
                num_scalar_prefetch=1, grid=(nblocks // together,), in_specs=in_specs,
                out_specs=out_specs, scratch_shapes=scratch,
            ),
            cost_estimate=pl.CostEstimate(
                flops=50_000_000 * slots * rows,
                bytes_accessed=20 << 20,
                transcendentals=nblocks * H * BLK * slots * rows,
            ),
        )(table, *[source] * (slots * together), query_t, *state, w_key, w_value_t, *finish)

    def partner_block(together, offset, slot, b, partner):
        at = b * together + offset
        return (where_to(partner[at // blocks_y, at % blocks_y, slot]), 0, 0)

    def edge_block(together, offset, slot, b, _):
        at = b * together + offset
        row, col = at // blocks_y, at % blocks_y
        if slot == 0:
            return (jnp.where(row == blocks_x - 1, blocks_y + col, col), 0, 0)
        return (2 * blocks_y + jnp.where(col == blocks_y - 1, blocks_x + row, row), 0, 0)

    state = add_keys(arrived[0], SPLIT[0], TOGETHER[0], NEXP, partners, partner_block, state)
    edge_blocks = jnp.concatenate(edges_in, axis=0)
    state = add_keys(edge_blocks, BLK, TOGETHER[0], 2, far_live, edge_block, state)
    state = add_keys(arrived[1], SPLIT[1], TOGETHER[1], NEXP, partners, partner_block, state)
    node_out = add_keys(
        arrived[2], SPLIT[2], TOGETHER[2], NEXP, partners, partner_block, state,
        (flat, w_out),
    )

    own_score = (
        jnp.sum((virt_query.astype(F32) * virt_key.astype(F32)).reshape(NVIRT, H, HD), axis=-1) * scale
    )
    own_score = jnp.repeat(own_score, HD, axis=1)
    part = virt_part
    ways = (
        ("col", mesh_cols, 1, 2),
        ("col", mesh_cols, 2, mesh_cols // 2),
        ("row", mesh_rows, 4, mesh_rows // 4),
        ("row", mesh_rows, 1, 4),
    )
    for stage, (axis, count, stride, size) in enumerate(ways):
        parts = [part] + [
            lax.ppermute(part, axis, [(i, turn(i, stride, size, shift)) for i in range(count)])
            for shift in range(1, size)
        ]
        if stage < len(ways) - 1:
            part = merge(in_order(parts, lax.axis_index(axis) // stride % size))
    own = jnp.concatenate([own_score, jnp.ones_like(own_score), virt_value.astype(F32)], axis=0)
    virt_out = pl.pallas_call(
        finish_kernel,
        name="finish",
        out_shape=shapes((NVIRT, D), F32),
        scratch_shapes=[pltpu.VMEM((len(parts), 3 * NVIRT, D), F32)],
        cost_estimate=pl.CostEstimate(flops=1 << 21, bytes_accessed=1 << 20, transcendentals=1 << 16),
    )(*parts, own, virt_emb, w_out)
    return node_out.reshape(feats.shape), virt_out


def solution(mesh):
    return jax.shard_map(
        shards,
        mesh=mesh,
        in_specs=(
            P("row", "col", None, None),
            P(),
            P(),
            P(),
            P(),
            P(),
            P("row", "col", None),
            P("row", "col", None),
            P("row", "col", None),
        ),
        out_specs=(P("row", "col", None, None), P()),
        check_vma=False,
    )
```

```python
import functools
import math

import jax
import jax.numpy as jnp
from jax import lax
from jax.experimental import pallas as pl
from jax.experimental.pallas import tpu as pltpu
from jax.sharding import PartitionSpec as P


D = 512
H = 8
HD = 64
BLK = 128
NEXP = 4
NVIRT = 4
PAIRS = H // 2
NEG_FILL = -1e30
SPLIT = (64, 32, 32)
TOGETHER = (2, 4, 4)
AXES = ("row", "col")
F32 = jnp.float32
BF16 = jnp.bfloat16


def dot_nt(a, b):
    return lax.dot_general(a, b, (((1,), (1,)), ((), ())), preferred_element_type=F32)


def dot_nn(a, b):
    return jnp.dot(a, b, preferred_element_type=F32)


def device_of(partner, blocks_x, blocks_y, mesh_cols):
    grid_cols = blocks_y * mesh_cols
    row, col = lax.div(partner, grid_cols * blocks_x), lax.div(lax.rem(partner, grid_cols), blocks_y)
    return row * mesh_cols + col


def send_kernel(first, sides, where_to, partners, feats, *refs):
    blocks_x, blocks_y = sides
    nblocks = blocks_x * blocks_y
    out, *edges = refs[:-3]
    held, in_sem, out_sem = refs[-3:]
    rows = out.shape[1]
    loads = [
        pltpu.make_async_copy(feats.at[block], held.at[block], in_sem.at[block])
        for block in range(nblocks)
    ]
    for load in loads:
        load.start()
    for block, load in enumerate(loads):
        load.wait()
        for m in range(NEXP):
            dest = where_to(partners[block // blocks_y, block % blocks_y, m])
            pltpu.make_async_copy(
                held.at[block, pl.ds(first, rows)], out.at[dest], out_sem.at[0]
            ).start()
    if edges:
        last_row, first_row, last_col, first_col = edges
        moves = [
            (held.at[pl.ds(nblocks - blocks_y, blocks_y)], last_row),
            (held.at[pl.ds(0, blocks_y)], first_row),
        ]
        for row in range(blocks_x):
            moves.append((held.at[row * blocks_y + blocks_y - 1], last_col.at[row]))
            moves.append((held.at[row * blocks_y], first_col.at[row]))
        copies = [
            pltpu.make_async_copy(kept, edge, out_sem.at[1 + index])
            for index, (kept, edge) in enumerate(moves)
        ]
        for copy in copies:
            copy.start()
        for copy in copies:
            copy.wait()
    every = out.at[pl.ds(0, nblocks * NEXP)]
    pltpu.make_async_copy(every, every, out_sem.at[0]).wait()


def pair_query(query_t, pair):
    both = query_t[pair * 2 * HD : (pair + 1) * 2 * HD, :]
    upper = lax.broadcasted_iota(jnp.int32, both.shape, 0) < HD
    zero = jnp.zeros_like(both)
    return jnp.concatenate([jnp.where(upper, both, zero), jnp.where(upper, zero, both)], axis=1)


def diagonal(mixed):
    return mixed[:HD, :BLK], mixed[HD:, BLK:]


def project_keys(rows, w_key, w_value_t, keys, values_t):
    gathered = rows[...]
    keys[...] = dot_nn(gathered, w_key[...]).astype(BF16)
    values_t[...] = dot_nt(w_value_t[...], gathered).astype(BF16)


def local_kernel(
    live, own, up, down, left, right, ids, w_query_t, w_key, w_value_t, virt_key, virt_value_t,
    virt_query, query_out, acc_out, top_out, total_out, virt_out, rows, keys, values_t,
    virt_top, virt_total, virt_acc,
):
    step = pl.program_id(0)
    sources = (own, up, down, left, right)
    for slot, source in enumerate(sources):
        rows[slot * BLK : (slot + 1) * BLK, :] = source[0]
    project_keys(rows, w_key, w_value_t, keys, values_t)
    query_t = (dot_nt(w_query_t[...], own[0]) * (1.0 / math.sqrt(HD))).astype(BF16)
    query_out[0] = query_t
    chosen = ids[0]
    chosen_pair = jnp.concatenate([chosen, chosen], axis=1)
    for pair in range(PAIRS):
        lanes = slice(pair * 2 * HD, (pair + 1) * 2 * HD)
        query = pair_query(query_t, pair)
        scores = dot_nn(keys[:, lanes], query)
        pieces = [scores[:BLK]]
        for slot in range(1, 5):
            alive = live[step // 4, step % 4, slot - 1] == 1
            pieces.append(jnp.where(alive, scores[slot * BLK : (slot + 1) * BLK], NEG_FILL))
        virt_scores = dot_nn(virt_key[:, lanes], query)
        member = lax.broadcasted_iota(jnp.int32, virt_scores.shape, 0) == chosen_pair
        virt_scores = jnp.where(member, virt_scores, NEG_FILL)
        top = jnp.max(virt_scores, axis=0, keepdims=True)
        for piece in pieces:
            top = jnp.maximum(top, jnp.max(piece, axis=0, keepdims=True))
        virt_shares = jnp.exp(virt_scores - top)
        total = jnp.sum(virt_shares, axis=0, keepdims=True)
        mixed = dot_nn(virt_value_t[lanes, :], virt_shares.astype(BF16))
        shares = [jnp.exp(piece - top) for piece in pieces]
        for share in shares:
            total = total + jnp.sum(share, axis=0, keepdims=True)
        weights = jnp.concatenate([share.astype(BF16) for share in shares], axis=0)
        mixed = mixed + dot_nn(values_t[lanes, :], weights)
        for half, part in enumerate(diagonal(mixed)):
            head = 2 * pair + half
            acc_out[0, head * HD : (head + 1) * HD, :] = part
            top_out[0, head : head + 1, :] = top[:, half * BLK : (half + 1) * BLK]
            total_out[0, head : head + 1, :] = total[:, half * BLK : (half + 1) * BLK]

    @pl.when(step == 0)
    def _():
        virt_top[...] = jnp.full_like(virt_top, NEG_FILL)
        virt_total[...] = jnp.zeros_like(virt_total)
        virt_acc[...] = jnp.zeros_like(virt_acc)

    scores = dot_nt(virt_query[...], keys[:BLK, :])
    member = lax.broadcasted_iota(jnp.int32, scores.shape, 0) // H == chosen
    scores = jnp.where(member, scores, NEG_FILL)
    before = virt_top[:, :1]
    top = jnp.maximum(before, jnp.max(scores, axis=1, keepdims=True))
    fade = jnp.exp(before - top)
    shares = jnp.where(member, jnp.exp(scores - top), 0.0)
    virt_top[...] = jnp.broadcast_to(top, virt_top.shape)
    virt_total[...] = virt_total[...] * fade + jnp.sum(shares, axis=1, keepdims=True)
    values = values_t[:, :BLK]
    gained = virt_acc[...] * fade
    for _ in range(3):
        rounded = shares.astype(BF16)
        gained = gained + dot_nt(rounded, values)
        shares = shares - rounded.astype(F32)
    virt_acc[...] = gained

    @pl.when(step == pl.num_programs(0) - 1)
    def _():
        head_of_lane = lax.broadcasted_iota(jnp.int32, (H, D), 1) // HD
        own_head = head_of_lane == lax.broadcasted_iota(jnp.int32, (H, D), 0)
        for v in range(NVIRT):
            heads = slice(v * H, (v + 1) * H)
            for kind, held in enumerate(
                (
                    jnp.broadcast_to(virt_top[heads, :1], (H, D)),
                    jnp.broadcast_to(virt_total[heads, :1], (H, D)),
                    virt_acc[heads, :],
                )
            ):
                row = kind * NVIRT + v
                virt_out[row : row + 1, :] = jnp.sum(
                    jnp.where(own_head, held, 0.0), axis=0, keepdims=True
                )


def remote_kernel(last, together, slots, table, *refs):
    masked = slots != NEXP
    step = pl.program_id(0)
    sources, refs = refs[: slots * together], refs[slots * together :]
    query_in, acc_in, top_in, total_in, w_key, w_value_t = refs[:6]
    refs = refs[6:]
    if last:
        feats, w_out, node_out, rows, keys, values_t, context = refs
    else:
        acc_out, top_out, total_out, rows, keys, values_t = refs
    count = sources[0].shape[1]
    for slot, source in enumerate(sources):
        rows[slot * count : (slot + 1) * count, :] = source[0]
    project_keys(rows, w_key, w_value_t, keys, values_t)
    for block in range(together):
        query_t = query_in[block]
        known = slice(block * slots * count, (block + 1) * slots * count)
        for pair in range(PAIRS):
            lanes = slice(pair * 2 * HD, (pair + 1) * 2 * HD)
            query = pair_query(query_t, pair)
            scores = dot_nn(keys[known, lanes], query)
            if masked:
                alive = [table[slots * (step * together + block) + slot] == 1 for slot in range(slots)]
                scores = jnp.concatenate(
                    [
                        jnp.where(alive[slot], scores[slot * count : (slot + 1) * count], NEG_FILL)
                        for slot in range(slots)
                    ],
                    axis=0,
                )
            pick = slice(2 * pair, 2 * pair + 1)
            pick_next = slice(2 * pair + 1, 2 * pair + 2)
            before = jnp.concatenate([top_in[block, pick, :], top_in[block, pick_next, :]], axis=1)
            total = jnp.concatenate(
                [total_in[block, pick, :], total_in[block, pick_next, :]], axis=1
            )
            top = jnp.maximum(before, jnp.max(scores, axis=0, keepdims=True))
            fade = jnp.exp(before - top)
            shares = jnp.exp(scores - top)
            total = total * fade + jnp.sum(shares, axis=0, keepdims=True)
            mixed = dot_nn(values_t[lanes, known], shares.astype(BF16))
            for half, part in enumerate(diagonal(mixed)):
                head = 2 * pair + half
                nodes = slice(half * BLK, (half + 1) * BLK)
                features = slice(head * HD, (head + 1) * HD)
                gained = acc_in[block, features, :] * fade[:, nodes] + part
                if last:
                    context[features, block * BLK : (block + 1) * BLK] = (
                        gained / total[:, nodes]
                    ).astype(BF16)
                else:
                    acc_out[block, features, :] = gained
                    top_out[block, head : head + 1, :] = top[:, nodes]
                    total_out[block, head : head + 1, :] = total[:, nodes]
    if last:
        mixed = lax.dot_general(
            context[...], w_out[...], (((0,), (0,)), ((), ())), preferred_element_type=F32
        )
        node_out[...] = (feats[...].astype(F32) + mixed.reshape(feats.shape)).astype(BF16)


def turn(index, stride, size, shift):
    place = index // stride % size
    return index + ((place + shift) % size - place) * stride


def in_order(parts, place):
    size = len(parts)
    ordered = []
    for source in range(size):
        chosen = parts[0]
        for shift in range(1, size):
            chosen = jnp.where((place - source) % size == shift, parts[shift], chosen)
        ordered.append(chosen)
    return ordered


def finish_kernel(*refs):
    parts, (own, virt_emb, w_out, virt_out, held) = refs[:-5], refs[-5:]
    size = len(parts)
    place = lax.rem(lax.axis_index("row"), size)
    for shift, part in enumerate(parts):
        held[lax.rem(place + (size - shift), size)] = part[...]
    every = [held.at[source] for source in range(size)] + [own]
    top = functools.reduce(jnp.maximum, [one[:NVIRT] for one in every])
    total, accum = jnp.zeros_like(top), jnp.zeros_like(top)
    for one in every:
        fade = jnp.exp(one[:NVIRT] - top)
        total = total + one[NVIRT : 2 * NVIRT] * fade
        accum = accum + one[2 * NVIRT :] * fade
    context = (accum / total).astype(BF16)
    virt_out[...] = virt_emb[...].astype(F32) + dot_nn(context, w_out[...])


def merge(parts):
    tops = [part[:NVIRT] for part in parts]
    top = functools.reduce(jnp.maximum, tops)
    fades = [jnp.exp(one - top) for one in tops]
    sums = [
        sum(part[kind * NVIRT : (kind + 1) * NVIRT] * fade for part, fade in zip(parts, fades))
        for kind in (1, 2)
    ]
    return jnp.concatenate([top, *sums], axis=0)


def halo(last_row, first_row, last_col, first_col):
    count_x, count_y = lax.axis_size("row"), lax.axis_size("col")

    def shift(edge, axis, count, step):
        pairs = [(i, i + step) for i in range(count) if 0 <= i + step < count]
        return lax.ppermute(edge, axis, pairs)

    return (
        shift(last_row, "row", count_x, 1),
        shift(first_row, "row", count_x, -1),
        shift(last_col, "col", count_y, 1),
        shift(first_col, "col", count_y, -1),
    )


def shards(feats, virt_emb, w_query, w_key, w_value, w_out, link_mask, partners, virt_ids):
    blocks_x, blocks_y = feats.shape[0], feats.shape[1]
    nblocks = blocks_x * blocks_y
    mesh_rows, mesh_cols = lax.axis_size("row"), lax.axis_size("col")
    devices = mesh_rows * mesh_cols
    where_to = functools.partial(
        device_of, blocks_x=blocks_x, blocks_y=blocks_y, mesh_cols=mesh_cols
    )
    flat = feats.reshape(nblocks, BLK, D)
    shapes = jax.ShapeDtypeStruct
    anywhere = pl.BlockSpec(memory_space=pl.ANY)

    outgoing = []
    first = 0
    for part, rows in enumerate(SPLIT):
        sides = (blocks_y, blocks_y, blocks_x, blocks_x) if part == 1 else ()
        out_shape = [shapes((devices, rows, D), BF16), *(shapes((n, BLK, D), BF16) for n in sides)]
        slots, *edges = pl.pallas_call(
            functools.partial(send_kernel, first, (blocks_x, blocks_y), where_to),
            out_shape=out_shape,
            in_specs=[pl.BlockSpec(memory_space=pltpu.SMEM), anywhere],
            out_specs=[anywhere] * len(out_shape),
            scratch_shapes=[
                pltpu.VMEM((nblocks, BLK, D), BF16),
                pltpu.SemaphoreType.DMA((nblocks,)),
                pltpu.SemaphoreType.DMA((3 + 2 * blocks_x,)),
            ],
            cost_estimate=pl.CostEstimate(flops=0, bytes_accessed=10 << 20, transcendentals=0),
        )(partners, flat)
        outgoing.append(slots)
        first += rows
        if edges:
            edges_in = halo(*edges)
    arrived = []
    for part, slots in enumerate(outgoing):
        arrived.append(lax.all_to_all(slots, AXES, split_axis=0, concat_axis=0, tiled=True))

    w_query_t, w_value_t = w_query.T, w_value.T
    scale = 1.0 / math.sqrt(HD)
    virt_rows = jnp.dot(
        virt_emb, jnp.concatenate([w_query, w_key, w_value], axis=1), preferred_element_type=F32
    ).astype(BF16)
    virt_query, virt_key, virt_value = virt_rows[:, :D], virt_rows[:, D : 2 * D], virt_rows[:, 2 * D :]
    pad_to = 8
    virt_key_rows = jnp.pad(virt_key, ((0, pad_to - NVIRT), (0, 0)))
    virt_value_cols = jnp.pad(virt_value, ((0, pad_to - NVIRT), (0, 0))).T
    head_of_lane = jnp.arange(D) // HD
    own_head = head_of_lane[None, :] == jnp.arange(H)[:, None]
    virt_query_rows = jnp.where(
        own_head[None], virt_query[:, None, :] * jnp.asarray(scale, BF16), jnp.zeros((), BF16)
    ).reshape(NVIRT * H, D)

    row_ids = lax.axis_index("row") * blocks_x + jnp.arange(blocks_x, dtype=jnp.int32)[:, None]
    col_ids = lax.axis_index("col") * blocks_y + jnp.arange(blocks_y, dtype=jnp.int32)[None, :]
    inside = jnp.stack(
        [
            jnp.broadcast_to(row_ids > 0, (blocks_x, blocks_y)),
            jnp.broadcast_to(row_ids < mesh_rows * blocks_x - 1, (blocks_x, blocks_y)),
            jnp.broadcast_to(col_ids > 0, (blocks_x, blocks_y)),
            jnp.broadcast_to(col_ids < mesh_cols * blocks_y - 1, (blocks_x, blocks_y)),
        ],
        axis=-1,
    )
    live = (link_mask == 1) & inside
    at_x, at_y = jnp.arange(blocks_x)[:, None], jnp.arange(blocks_y)[None, :]
    outer = (at_x == 0, at_x == blocks_x - 1, at_y == 0, at_y == blocks_y - 1)
    far = jnp.stack([jnp.broadcast_to(side, (blocks_x, blocks_y)) for side in outer], axis=-1)
    near_live = (live & ~far).astype(jnp.int32)
    far_live = (live & far).reshape(nblocks, 2, 2).any(axis=-1).astype(jnp.int32).reshape(-1)

    def above(b, *_):
        return (jnp.where(b < blocks_y, b, b - blocks_y), 0, 0)

    def below(b, *_):
        return (jnp.where(b >= nblocks - blocks_y, b, b + blocks_y), 0, 0)

    def before(b, *_):
        return (jnp.where(b % blocks_y == 0, b, b - 1), 0, 0)

    def after(b, *_):
        return (jnp.where(b % blocks_y == blocks_y - 1, b, b + 1), 0, 0)

    def same(b, *_):
        return (b, 0, 0)

    def whole(shape):
        return pl.BlockSpec(shape, lambda b, *_: (0,) * len(shape))

    block = (1, BLK, D)
    turned = (1, D, BLK)
    stats = (1, H, BLK)
    weight = whole((D, D))
    state_shapes = [
        shapes((nblocks, D, BLK), F32), shapes((nblocks, H, BLK), F32), shapes((nblocks, H, BLK), F32)
    ]
    state_specs = [pl.BlockSpec(turned, same), pl.BlockSpec(stats, same), pl.BlockSpec(stats, same)]
    local_keys = 5 * BLK
    query_t, *state, virt_part = pl.pallas_call(
        local_kernel,
        name="local",
        out_shape=[shapes((nblocks, D, BLK), BF16), *state_shapes, shapes((3 * NVIRT, D), F32)],
        grid_spec=pltpu.PrefetchScalarGridSpec(
            num_scalar_prefetch=1,
            grid=(nblocks,),
            in_specs=[
                *(pl.BlockSpec(block, index) for index in (same, above, below, before, after)),
                pl.BlockSpec((1, 1, BLK), same),
                weight, weight, weight,
                whole((pad_to, D)), whole((D, pad_to)), whole((NVIRT * H, D)),
            ],
            out_specs=[pl.BlockSpec(turned, same), *state_specs, whole((3 * NVIRT, D))],
            scratch_shapes=[
                pltpu.VMEM((local_keys, D), BF16),
                pltpu.VMEM((local_keys, D), BF16),
                pltpu.VMEM((D, local_keys), BF16),
                pltpu.VMEM((NVIRT * H, BLK), F32),
                pltpu.VMEM((NVIRT * H, BLK), F32),
                pltpu.VMEM((NVIRT * H, D), F32),
            ],
        ),
        cost_estimate=pl.CostEstimate(
            flops=40_000_000_000, bytes_accessed=30 << 20, transcendentals=nblocks * H * BLK * local_keys
        ),
    )(
        near_live, flat, flat, flat, flat, flat, virt_ids.reshape(nblocks, 1, BLK),
        w_query_t, w_key, w_value_t, virt_key_rows, virt_value_cols, virt_query_rows,
    )

    def add_keys(source, rows, together, slots, table, index, state, finish=()):
        def blocks_of(*shape):
            return pl.BlockSpec((together, *shape), same)

        states = [blocks_of(D, BLK), blocks_of(H, BLK), blocks_of(H, BLK)]
        in_specs = [
            *(
                pl.BlockSpec((1, rows, D), functools.partial(index, together, offset, slot))
                for offset in range(together)
                for slot in range(slots)
            ),
            blocks_of(D, BLK), *states, weight, weight,
        ]
        count = together * slots * rows
        scratch = [
            pltpu.VMEM((count, D), BF16), pltpu.VMEM((count, D), BF16), pltpu.VMEM((D, count), BF16)
        ]
        if finish:
            in_specs += [blocks_of(BLK, D), weight]
            out_shape, out_specs = shapes(flat.shape, BF16), blocks_of(BLK, D)
            scratch += [pltpu.VMEM((D, together * BLK), BF16)]
        else:
            out_shape, out_specs = state_shapes, states
        return pl.pallas_call(
            functools.partial(remote_kernel, bool(finish), together, slots),
            out_shape=out_shape,
            grid_spec=pltpu.PrefetchScalarGridSpec(
                num_scalar_prefetch=1, grid=(nblocks // together,), in_specs=in_specs,
                out_specs=out_specs, scratch_shapes=scratch,
            ),
            cost_estimate=pl.CostEstimate(
                flops=50_000_000 * slots * rows,
                bytes_accessed=20 << 20,
                transcendentals=nblocks * H * BLK * slots * rows,
            ),
        )(table, *[source] * (slots * together), query_t, *state, w_key, w_value_t, *finish)

    def partner_block(together, offset, slot, b, partner):
        at = b * together + offset
        return (where_to(partner[at // blocks_y, at % blocks_y, slot]), 0, 0)

    def edge_block(together, offset, slot, b, _):
        at = b * together + offset
        row, col = at // blocks_y, at % blocks_y
        if slot == 0:
            return (jnp.where(row == blocks_x - 1, blocks_y + col, col), 0, 0)
        return (2 * blocks_y + jnp.where(col == blocks_y - 1, blocks_x + row, row), 0, 0)

    state = add_keys(arrived[0], SPLIT[0], TOGETHER[0], NEXP, partners, partner_block, state)
    edge_blocks = jnp.concatenate(edges_in, axis=0)
    state = add_keys(edge_blocks, BLK, 4, 2, far_live, edge_block, state)
    state = add_keys(arrived[1], SPLIT[1], TOGETHER[1], NEXP, partners, partner_block, state)
    node_out = add_keys(
        arrived[2], SPLIT[2], TOGETHER[2], NEXP, partners, partner_block, state,
        (flat, w_out),
    )

    own_score = (
        jnp.sum((virt_query.astype(F32) * virt_key.astype(F32)).reshape(NVIRT, H, HD), axis=-1) * scale
    )
    own_score = jnp.repeat(own_score, HD, axis=1)
    part = virt_part
    ways = (
        ("col", mesh_cols, 1, 2),
        ("col", mesh_cols, 2, mesh_cols // 2),
        ("row", mesh_rows, 4, mesh_rows // 4),
        ("row", mesh_rows, 1, 4),
    )
    for stage, (axis, count, stride, size) in enumerate(ways):
        parts = [part] + [
            lax.ppermute(part, axis, [(i, turn(i, stride, size, shift)) for i in range(count)])
            for shift in range(1, size)
        ]
        if stage < len(ways) - 1:
            part = merge(in_order(parts, lax.axis_index(axis) // stride % size))
    own = jnp.concatenate([own_score, jnp.ones_like(own_score), virt_value.astype(F32)], axis=0)
    virt_out = pl.pallas_call(
        finish_kernel,
        name="finish",
        out_shape=shapes((NVIRT, D), F32),
        scratch_shapes=[pltpu.VMEM((len(parts), 3 * NVIRT, D), F32)],
        cost_estimate=pl.CostEstimate(flops=1 << 21, bytes_accessed=1 << 20, transcendentals=1 << 16),
    )(*parts, own, virt_emb, w_out)
    return node_out.reshape(feats.shape), virt_out


def solution(mesh):
    return jax.shard_map(
        shards,
        mesh=mesh,
        in_specs=(
            P("row", "col", None, None),
            P(),
            P(),
            P(),
            P(),
            P(),
            P("row", "col", None),
            P("row", "col", None),
            P("row", "col", None),
        ),
        out_specs=(P("row", "col", None, None), P()),
        check_vma=False,
    )
```
